32 devices in a mesh: group: 2 (over y), tensor: 8 (over z, core), seq: 2 (over x).
Axes of the slice: x: 2, y: 2, z: 4, core: 2. Of those that a mesh axis runs over, the one named last changes fastest.
Arguments:
- hidden_states: bfloat16 [512, 2048], P(('group', 'tensor', 'seq')), may hold values from -200 to 200, as said below
- norm_gain: bfloat16 [2048], replicated, may hold values from 0.099609375 to 1.8984375
- expert_ids: int32 [512, 8], P(('group', 'tensor', 'seq')), may hold values from 0 to 15, all different within a row; in each aligned block of 16 rows (0 to 15, 16 to 31, ...) at most 16 rows name the same one
- route_weights: float32 [512, 8], P(('group', 'tensor', 'seq')), may hold values from 0.05 to 1
- w_gate: bfloat16 [16, 2048, 768], P(('group', 'tensor'), None, 'seq'), may hold values from -0.125 to 0.125
- w_up: bfloat16 [16, 2048, 768], P(('group', 'tensor'), None, 'seq'), may hold values from -0.125 to 0.125
- w_down: bfloat16 [16, 768, 2048], P(('group', 'tensor'), 'seq'), may hold values from -0.21875 to 0.21875
- prefill_key_value: bfloat16 [4, 16, 4, 4096, 256], P('seq', None, None, ('group', 'tensor')), may hold values from -6 to 6
- lengths: int32 [16], replicated, may hold values from 1 to 4096, 49152 in all
Outputs:
- moe_out: bfloat16 [512, 2048], P(('group', 'tensor', 'seq'))
- decoder_slot_cache: bfloat16 [4, 64, 4096, 256], P('seq', 'tensor', 'group')
The draws below stay inside these ranges and needn't reach their ends.
Inputs may be any that keep to these rules, and one draw needn't show every extreme that they name: `hidden_states`: hidden states of rows and features of differing scales. `expert_ids`: each row names 8 different experts; in the 16 rows of one device (aligned blocks) no expert is named by more than 16 rows, a bound that some block reaches. `lengths`: the longest request has exactly 4096 cached positions.
All inputs are finite; a program needn't handle non-finite values.
Results may differ from the reference program's by a relative error of at most 0.0079.
Values may be sent and summed in bfloat16 or wider, within the bound.
A program may use at most 128 MiB of HBM per device.

```python
import math
import jax
import jax.numpy as jnp
import numpy as np
from jax import lax

D = 2048
KEY_VALUE_HEADS = 4
HEAD_DIM = 128
EXP_FF = 768
TOP = 8
TOK_DEV = 16
HANDOVER_LAYERS = 4
REQUEST_COUNT = 16
CONTEXT_SPAN = 4096
EXPERTS = 16
TOKENS = 512
SLOT_CAP = 16
HID_PART = 384


def draw_hidden_states(key, part):
    keys = jax.random.split(key, 3)
    base = jnp.clip(jax.random.normal(keys[0], (TOKENS, D), jnp.float32), -4.0, 4.0)
    rows = jnp.exp(jax.random.uniform(keys[2], (TOKENS, 1), jnp.float32, 0.0, math.log(10.0)))
    columns = jnp.exp(jax.random.uniform(keys[1], (1, D), jnp.float32, math.log(0.3), math.log(3.0)))
    return (base * columns * rows).astype(jnp.bfloat16)


def block_scale(own_key, extent, cuts, smallest, largest):
    def one(position, shards_of):
        steps = jax.random.uniform(jax.random.fold_in(jax.random.fold_in(own_key, 6), position), (shards_of,), jnp.float32, smallest / len(cuts), largest / len(cuts))
        return jnp.repeat(jnp.exp(steps), extent[position] // shards_of).reshape((-1,) + (1,) * (len(extent) - position - 1))

    loudness = one(*cuts[0])
    for cut in cuts[1:]:
        loudness = loudness * one(*cut)
    return loudness


def split_up(number_of, total, limit, skew):
    weights = [(1 << 20) // math.isqrt(rank ** skew) + 1 for rank in range(2, number_of + 1)]
    spare, holding = total - limit - (number_of - 1), [1] * (number_of - 1)
    while spare > 0:
        movable = [i for i in range(number_of - 1) if holding[i] < limit]
        pool, remaining = sum([weights[i] for i in movable]), spare
        for i in movable:
            more = min(limit - holding[i], max(1, remaining * weights[i] // pool), spare)
            holding[i] = holding[i] + more
            spare = spare - more
    return np.array([limit] + holding)


def uneven(rng, amount, total, most, slope):
    if amount == 2:
        one = jax.random.randint(rng, (), max(1, total - most), min(most, total - 1) + 1)
        return jnp.stack([one, total - one])
    tallies = jnp.asarray(split_up(amount, total, most, slope), jnp.int32)
    pairs = (amount - 1) // 2
    giver, taker = tallies[1:1 + 2 * pairs:2], tallies[2:2 + 2 * pairs:2]
    room = jnp.minimum(giver - 1, most - taker)
    shifted = jax.random.randint(jax.random.fold_in(rng, 1), (pairs,), 0, 1 << 20) % (room + 1)
    tallies = tallies.at[1:1 + 2 * pairs:2].set(giver - shifted).at[2:2 + 2 * pairs:2].set(taker + shifted)
    return tallies[jax.random.permutation(jax.random.fold_in(rng, 2), amount)]


def shared_out(rng, own, number, rows, number_of, top, bound, slope):
    ranking = jax.random.permutation(rng, number_of)
    heavy_load, usual = load_shares(number_of, rows * top, bound, slope, True), load_shares(number_of, rows * top, bound, slope, False)
    places = jnp.arange(number_of)

    def named(sizes, turn):
        used = int((sizes > 0).sum())
        fixed = max(1, used // 4)
        shifted = fixed + (places - fixed + turn * (used - fixed)) % max(1, number_of - fixed)
        return jnp.zeros((number_of,), jnp.int32).at[ranking[jnp.where(places < fixed, places, shifted)]].set(jnp.asarray(sizes, jnp.int32))

    sizes = jnp.where(number % 4 == 0, named(heavy_load, number // 4), named(usual, number - number // 4 - 1))
    mixed = jax.random.permutation(jax.random.fold_in(own, 3), number_of)
    giver, sink = mixed[0:number_of // 2 * 2:2], mixed[1:number_of // 2 * 2:2]
    margin = jnp.minimum(sizes[giver] - 1, bound - sizes[sink]) // 2
    margin = jnp.where((giver == ranking[0]) | (sink == ranking[0]) | (sizes[sink] == 0), 0, jnp.maximum(margin, 0))
    shifted = jax.random.randint(jax.random.fold_in(own, 4), (number_of // 2,), 0, 1 << 20) % (margin + 1)
    sizes = sizes.at[giver].add(-shifted).at[sink].add(shifted)
    members = jnp.searchsorted(jnp.cumsum(sizes), jnp.arange(rows * top), side="right").astype(jnp.int32)
    grid = members.reshape(top, rows).T
    grid = grid[jax.random.permutation(jax.random.fold_in(own, 1), rows)]
    turn = jax.random.randint(jax.random.fold_in(own, 2), (rows, 1), 0, top)
    return jnp.take_along_axis(grid, (jnp.arange(top)[None, :] + turn) % top, axis=1)


def load_shares(amount, total, bound, slope, full):
    portions = [(1 << 20) // math.isqrt(standing ** slope) + 1 for standing in range(1, amount + 1)]
    largest = bound if full else min(bound, max(-(-total // amount), total * portions[0] // sum(portions)))
    least = 1 if total - largest >= amount - 1 else 0
    holding, spare = [largest] + [least] * (amount - 1), total - largest - least * (amount - 1)
    while spare > 0:
        candidates = [i for i in range(1, amount) if holding[i] < largest] or [i for i in range(1, amount) if holding[i] < bound]
        pool, left = sum([portions[i] for i in candidates]), spare
        for i in candidates:
            extra = min(bound - holding[i], max(1, left * portions[i] // pool), spare)
            holding[i] = holding[i] + extra
            spare = spare - extra
    return np.array(holding)


def gaussian(stream_key, dims, scale, most, cuts=(), kind=jnp.bfloat16):
    values = jax.random.normal(stream_key, dims, jnp.float32) * scale
    if len(cuts) > 0:
        values = block_scale(stream_key, dims, cuts, -0.22, 0.18) * values
    return jnp.clip(values, min=-most, max=most).astype(kind)


def setup_inputs(seed: int = 0) -> dict:
    arg_keys = jax.random.split(jax.random.key(seed), 10)
    hidden_states = draw_hidden_states(jax.random.fold_in(arg_keys[9], 71), 0)
    norm_gain = jnp.clip(1.0 + 0.18 * jax.random.normal(arg_keys[1], (D,), jnp.float32), 0.099609375, 1.8984375).astype(jnp.bfloat16)
    expert_ids_keys = jax.random.split(jax.random.fold_in(arg_keys[2], 1), TOKENS // TOK_DEV)
    expert_ids_turns = jax.random.permutation(jax.random.fold_in(arg_keys[2], 3), TOKENS // TOK_DEV)
    expert_ids = jax.vmap(lambda own, number: shared_out(jax.random.fold_in(arg_keys[2], 2), own, number, TOK_DEV, EXPERTS, TOP, SLOT_CAP, 2))(expert_ids_keys, expert_ids_turns).reshape((TOKENS, TOP))
    route_weights = jnp.clip(jnp.exp(math.log(1.0) - 2.9957323 * jax.random.uniform(arg_keys[3], (TOKENS, TOP), jnp.float32) ** block_scale(arg_keys[3], (TOKENS, TOP), ((0, 32),), -0.2, 0.2)), 0.05, 1.0)
    w_gate = gaussian(arg_keys[4], (EXPERTS, D, EXP_FF), D ** -0.5, 0.125, ((0, 16), (2, 2)))
    w_up = gaussian(arg_keys[5], (EXPERTS, D, EXP_FF), D ** -0.5, 0.125, ((0, 16), (2, 2)))
    w_down = gaussian(arg_keys[6], (EXPERTS, EXP_FF, D), EXP_FF ** -0.5, 0.21875, ((0, 16), (1, 2)))
    prefill_key_value = gaussian(arg_keys[7], (HANDOVER_LAYERS, REQUEST_COUNT, KEY_VALUE_HEADS, CONTEXT_SPAN, 2 * HEAD_DIM), 1.0, 6.0, ((0, 2), (3, 16)))
    lengths = uneven(arg_keys[8], REQUEST_COUNT, REQUEST_COUNT * CONTEXT_SPAN * 3 // 4, CONTEXT_SPAN, 1).astype(jnp.int32)
    return dict(hidden_states=hidden_states, norm_gain=norm_gain, expert_ids=expert_ids, route_weights=route_weights, w_gate=w_gate, w_up=w_up, w_down=w_down, prefill_key_value=prefill_key_value, lengths=lengths)


def reference(hidden_states, norm_gain, expert_ids, route_weights, w_gate, w_up, w_down, prefill_key_value, lengths):
    wide = hidden_states.astype(jnp.float32)
    scale = lax.rsqrt(lax.optimization_barrier(jnp.mean(wide * wide, axis=1, keepdims=True)) + 1e-06)
    normed = (wide * scale * norm_gain.astype(jnp.float32)).astype(jnp.bfloat16)
    share = route_weights / lax.optimization_barrier(jnp.sum(route_weights, axis=1, keepdims=True))
    flat_ids = expert_ids.reshape(-1)
    flat_share = share.reshape(-1)
    owners = jnp.arange(TOKENS * TOP, dtype=jnp.int32) // TOP
    capacity = TOKENS // TOK_DEV * SLOT_CAP
    slot_numbers = jnp.arange(capacity, dtype=jnp.int32)

    def one_expert(carry, inputs):
        index, gate_w, up_w, down_w = inputs
        matches = flat_ids == index
        count = jnp.sum(matches.astype(jnp.int32))
        picks = jnp.nonzero(matches, size=capacity, fill_value=0)[0].astype(jnp.int32)
        valid = slot_numbers < count
        weight = jnp.where(valid, flat_share[picks], jnp.zeros((), flat_share.dtype))
        rows = normed[owners[picks]]
        gate = jnp.dot(rows, gate_w, preferred_element_type=jnp.float32)
        upper = jnp.dot(rows, up_w, preferred_element_type=jnp.float32)
        active = (jax.nn.silu(gate) * upper).astype(jnp.bfloat16)
        total = jnp.zeros((capacity, D), jnp.float32)
        for block in range(EXP_FF // HID_PART):
            lower = block * HID_PART
            part = jnp.dot(active[:, lower:lower + HID_PART], down_w[lower:lower + HID_PART, :], preferred_element_type=jnp.float32)
            part = lax.optimization_barrier(part.astype(jnp.bfloat16))
            total = total + part.astype(jnp.float32)
        result = lax.optimization_barrier(total.astype(jnp.bfloat16)).astype(jnp.float32)
        carry = carry.at[owners[picks]].add(weight[:, None] * result)
        return (carry, None)
    start = jnp.zeros((TOKENS, D), jnp.float32)
    summed, _ = lax.scan(one_expert, start, (jnp.arange(EXPERTS, dtype=jnp.int32), w_gate, w_up, w_down))
    moe_out = summed.astype(jnp.bfloat16)
    positions = jnp.arange(CONTEXT_SPAN, dtype=jnp.int32)
    keep = positions[None, :] < lengths[:, None]
    masked_entries = jnp.where(keep[None, :, None, :, None], prefill_key_value, jnp.zeros((), prefill_key_value.dtype))
    decoder_slot_cache = masked_entries.reshape(HANDOVER_LAYERS, REQUEST_COUNT * KEY_VALUE_HEADS, CONTEXT_SPAN, 2 * HEAD_DIM)
    return (moe_out, decoder_slot_cache)
```

```python
import functools
import jax
import jax.numpy as jnp
from jax import lax
from jax.experimental import pallas as pl
from jax.experimental.pallas import tpu as pltpu
from jax.sharding import PartitionSpec as P

epsilon = 1e-06
LANES = 128
DENSE_TOKENS = 1024
WINDOW = 3
LINE = 8
LAG = 3
UNIT = 32
DEEP = 32
PLANS = (
    (48, 44, 36, 32, 48, 44, 36, 32),
    (56, 48, 44, 44, 64, 56, 40, 32),
    (64, 60, 52, 48, 64, 64, 56, 40),
    (64, 64, 64, 64, 64, 64, 64, 64),
)
MESH = pl.DeviceIdType.MESH


def hand_over(prefill_key_value, lengths):
    layers_here, requests, heads, block, width = prefill_key_value.shape
    block_index = lax.axis_index("group") * lax.axis_size("tensor") + lax.axis_index("tensor")
    positions = block_index * block + jnp.arange(block, dtype=jnp.int32)
    keep = positions[None, :] < lengths[:, None]
    masked_entries = jnp.where(
        keep[None, :, None, :, None], prefill_key_value, jnp.zeros((), prefill_key_value.dtype)
    )
    flat = masked_entries.reshape(layers_here, requests * heads, block, width)
    return lax.all_to_all(flat, "tensor", split_axis=1, concat_axis=2, tiled=True)


def mixture(hidden_states, norm_gain, expert_ids, route_weights, w_gate, w_up, w_down):
    wide = hidden_states.astype(jnp.float32)
    scale = lax.rsqrt(jnp.mean(wide * wide, axis=1, keepdims=True) + epsilon)
    normed = (wide * scale * norm_gain.astype(jnp.float32)).astype(jnp.bfloat16)
    share = route_weights / jnp.sum(route_weights, axis=1, keepdims=True)
    expert_local, model_width, part_width = w_gate.shape
    sources = lax.axis_size("group") * lax.axis_size("tensor")
    experts = expert_local * sources
    rows_here, top_count = expert_ids.shape
    most = min(rows_here, max(2, 2 * rows_here * top_count // experts))
    flat_ids = expert_ids.reshape(-1)
    expert_grid = jnp.arange(experts, dtype=jnp.int32)
    onehot = (flat_ids[:, None] == expert_grid[None, :]).astype(jnp.int32)
    choices = jnp.arange(flat_ids.shape[0], dtype=jnp.int32)
    before = (choices[:, None] > choices[None, :]).astype(jnp.float32)
    earlier = jnp.dot(before, onehot.astype(jnp.float32), preferred_element_type=jnp.float32).astype(jnp.int32)
    position = jnp.sum(earlier * onehot, axis=1)
    target = flat_ids * most + position
    slot_grid = jnp.arange(experts * most, dtype=jnp.int32)
    hits = (target[:, None] == slot_grid[None, :]).reshape(rows_here, top_count, experts * most)
    select = jnp.sum(hits.astype(jnp.float32), axis=1).astype(jnp.bfloat16)
    mixing = jnp.sum(jnp.where(hits, share[:, :, None], 0.0), axis=1)
    outgoing = lax.dot_general(
        select, normed, (((0,), (0,)), ((), ())), preferred_element_type=jnp.float32
    )
    outgoing = outgoing.astype(jnp.bfloat16).reshape(experts, most, model_width)
    arrived = lax.all_to_all(outgoing, ("group", "tensor"), split_axis=0, concat_axis=0, tiled=True)
    arrived = arrived.reshape(sources, expert_local, most, model_width)
    pooled = lax.all_gather(arrived, "seq", axis=0, tiled=True)
    gate = jnp.einsum("semd,edf->semf", pooled, w_gate, preferred_element_type=jnp.float32)
    upper = jnp.einsum("semd,edf->semf", pooled, w_up, preferred_element_type=jnp.float32)
    active = (jax.nn.silu(gate) * upper).astype(jnp.bfloat16)
    summed = lax.psum_scatter(
        jnp.einsum("semf,efd->semd", active, w_down, preferred_element_type=jnp.float32).astype(
            jnp.bfloat16
        ),
        "seq",
        scatter_dimension=0,
        tiled=True,
    )
    returned = lax.all_to_all(
        summed.reshape(sources * expert_local, most, model_width),
        ("group", "tensor"),
        split_axis=0,
        concat_axis=0,
        tiled=True,
    )
    flat_back = returned.reshape(experts * most, model_width).astype(jnp.float32)
    mixed = jnp.dot(mixing, flat_back, precision=lax.Precision.HIGHEST)
    return mixed.astype(jnp.bfloat16)


def routed_shards(
    hidden_states, norm_gain, expert_ids, route_weights, w_gate, w_up, w_down, prefill_key_value, lengths
):
    moe_out = mixture(hidden_states, norm_gain, expert_ids, route_weights, w_gate, w_up, w_down)
    decoder_slot_cache = hand_over(prefill_key_value, lengths)
    return (moe_out, decoder_slot_cache)


def fused_kernel(
    sizes, caps, cuts,
    hidden_ref, gain_ref, ids_ref, weights_ref, gate_w, up_w, down_w, kv_ref, packed_ref,
    moe_ref, cache_ref, other_pool_ref,
    tokens, mixes, partial, gathered, folded, swapped, mate_out, mate_in, outgoing, returned,
    lend_first, lend_last,
    near_send, near_recv, far_send, far_recv, own_sem,
    stream_send, stream_recv, relay_send, share_send, share_recv, lend_send, lend_recv, lent_send, lent_recv,
    line_send, line_recv, pair_send, pair_recv, plane_send, plane_recv,
    part_send, part_recv, swap_send, swap_recv, mate_send, mate_recv, back_send, back_recv,
):
    groups, line, seqs = sizes
    plane = groups * seqs
    g, t, s = lax.axis_index("group"), lax.axis_index("tensor"), lax.axis_index("seq")
    here = g * seqs + s
    chips = line // 2
    chip, core = t // 2, lax.rem(t, 2)
    pair = (g, t + 1 - 2 * core, s)
    mate = chip + 1 - 2 * lax.rem(chip, 2)
    across, mate_across = lax.rem(chip + 2, chips), lax.rem(mate + 2, chips)
    mate_device, across_device = (g, mate * 2 + core, s), (g, across * 2 + core, s)
    layers, slots_all, block, _ = kv_ref.shape
    slots = slots_all // line
    rounds = layers * slots
    half_line = line // 2
    half, seat = t // half_line, lax.rem(t, half_line)
    far_half = 1 - half

    def in_line(step):
        other = lax.rem(t + step, line)
        return other, (g, other, s)

    def in_plane(step):
        other = lax.rem(here + step, plane)
        return other, (other // seqs, t, lax.rem(other, seqs))

    barrier = pltpu.get_barrier_semaphore()
    for step in range(1, line):
        pl.semaphore_signal(barrier, inc=1, device_id=in_line(step)[1], device_id_type=MESH)
    for step in range(1, plane):
        pl.semaphore_signal(barrier, inc=1, device_id=in_plane(step)[1], device_id_type=MESH)
    for k in range(half_line):
        pl.semaphore_signal(
            barrier, inc=1, device_id=(1 - g, far_half * half_line + k, s), device_id_type=MESH
        )

    columns = pl.ds(pl.multiple_of(t * block, block), block)
    own = pltpu.make_async_copy(
        kv_ref.at[:, pl.ds(t * slots, slots)], cache_ref.at[:, :, columns], own_sem
    )
    own.start()

    wide = hidden_ref[...].astype(jnp.float32)
    scale = lax.rsqrt(jnp.mean(wide * wide, axis=1, keepdims=True) + epsilon)
    tokens[here, chip, core] = (wide * scale * gain_ref[...].astype(jnp.float32)[None, :]).astype(jnp.bfloat16)
    top, rows = ids_ref.shape
    ids = ids_ref[...].T
    weights = weights_ref[...].T
    share = weights / jnp.sum(weights, axis=1, keepdims=True)
    lane = lax.broadcasted_iota(jnp.int32, (rows, LANES), 1)
    mix = jnp.zeros((rows, LANES), jnp.float32)
    for k in range(top):
        mix = mix + jnp.where(lane == ids[:, k : k + 1], share[:, k : k + 1], 0.0)
    mixes[here, chip, core] = mix

    pl.semaphore_wait(barrier, line + plane - 2 + half_line)

    def cap_of(device):
        total = 0
        for k in range(line):
            total = total + jnp.where(device == k, caps[k], 0)
        return total

    cap = cap_of(t)
    inner = jnp.logical_or(chip == 1, chip == 2)
    first_chip, last_chip = 1 + far_half * 1, far_half * 3
    lane_index = lax.rem(chip, 2)

    def pool(side, lane, entry):
        start = pl.multiple_of((side * DEEP + entry) * UNIT, UNIT)
        return cache_ref.at[:, pl.ds(lane * (slots // 2), slots // 2), pl.ds(start, UNIT)]

    def near_copy(index, step):
        other = half * half_line + lax.rem(seat + step, half_line)
        layer, slot = index // slots, lax.rem(index, slots)
        return pltpu.make_async_remote_copy(
            src_ref=kv_ref.at[layer, other * slots + slot],
            dst_ref=cache_ref.at[layer, slot, columns],
            send_sem=near_send.at[index, step],
            recv_sem=near_recv.at[index, step],
            device_id=(g, other, s),
            device_id_type=MESH,
        )

    def far_copy(layer, index, k, source):
        other = far_half * half_line + k
        slot = lax.rem(index, slots)
        kept = block - cuts[layer]
        return pltpu.make_async_remote_copy(
            src_ref=kv_ref.at[layer, other * slots + slot, pl.ds(0, kept)],
            dst_ref=cache_ref.at[layer, slot, pl.ds(pl.multiple_of(t * block, block), kept)],
            send_sem=far_send.at[index, k],
            recv_sem=far_recv.at[index, source],
            device_id=(g, other, s),
            device_id_type=MESH,
        )

    def stream_copy(place):
        entry = lax.rem(place + cap - DEEP, cap)
        first = entry < DEEP
        target = jnp.where(first, entry, entry - (cap - DEEP))
        return pltpu.make_async_remote_copy(
            src_ref=packed_ref.at[entry],
            dst_ref=pool(half, lane_index, target),
            send_sem=stream_send.at[entry],
            recv_sem=stream_recv.at[lane_index, target],
            device_id=(g, jnp.where(first, first_chip, last_chip) * 2 + core, s),
            device_id_type=MESH,
        )

    def share_copy(lane, entry):
        return pltpu.make_async_remote_copy(
            src_ref=pool(far_half, lane, entry), dst_ref=other_pool_ref.at[lane, entry],
            send_sem=share_send.at[lane, entry], recv_sem=share_recv.at[lane, entry],
            device_id=pair, device_id_type=MESH,
        )

    def relay_copy(lane, entry, target):
        return pltpu.make_async_remote_copy(
            src_ref=pool(far_half, lane, entry), dst_ref=pool(far_half, lane, target),
            send_sem=relay_send.at[lane, entry], recv_sem=stream_recv.at[lane, target],
            device_id=mate_device, device_id_type=MESH,
        )

    def span_of(amount, index):
        at = jnp.clip(index, 0, rounds)
        after = jnp.clip(index + 1, 0, rounds)
        return amount * at // rounds, amount * after // rounds

    lends = [buffer for buffer in (lend_first, lend_last)]

    def lend_copy(layer):
        cut = cuts[layer]
        return pltpu.make_async_remote_copy(
            src_ref=kv_ref.at[layer, pl.ds(far_half * half_line * slots, half_line * slots), pl.ds(block - cut, cut)],
            dst_ref=lends[layer],
            send_sem=lend_send.at[layer], recv_sem=lend_recv.at[layer],
            device_id=(1 - g, t, s), device_id_type=MESH,
        )

    def lent_copy(layer, k, source):
        cut = cuts[layer]
        start = pl.multiple_of(t * block + block - cut, 16)
        return pltpu.make_async_remote_copy(
            src_ref=lends[layer].at[pl.ds(k * slots, slots)],
            dst_ref=cache_ref.at[layer, :, pl.ds(start, cut)],
            send_sem=lent_send.at[layer, k], recv_sem=lent_recv.at[layer, source],
            device_id=(1 - g, far_half * half_line + k, s), device_id_type=MESH,
        )

    lent_layers = [layer for layer in range(layers) if cuts[layer] > 0]

    def kv_start(layer, index):
        for step in range(1, half_line):
            near_copy(index, step).start()

        @pl.when(g == 0)
        def _():
            for k in range(half_line):
                far_copy(layer, index, k, seat).start()

        @pl.when(g == 1)
        def _():
            @pl.loop(*span_of(cap, index))
            def _(place):
                stream_copy(place).start()

    def kv_sent(layer, index):
        for step in range(1, half_line):
            near_copy(index, step).wait_send()

        @pl.when(g == 0)
        def _():
            for k in range(half_line):
                far_copy(layer, index, k, seat).wait_send()

        @pl.when(g == 1)
        def _():
            @pl.loop(*span_of(cap, index))
            def _(place):
                stream_copy(place).wait_send()

    def arrivals(index):
        @pl.when(g == 1)
        def _():
            for i in range(2):
                amount = cap_of(far_half * half_line + 2 * i + core)

                @pl.loop(*span_of(amount, index - LAG))
                def _(place):
                    entry = lax.rem(place + amount - DEEP, amount)

                    @pl.when(jnp.logical_and(inner, entry < DEEP))
                    def _():
                        relay_copy(i, entry, entry).wait_recv()
                        share_copy(i, entry).start()

                        @pl.when(entry >= amount - DEEP)
                        def _():
                            relay_copy(i, entry, entry - (amount - DEEP)).start()

                    @pl.when(jnp.logical_and(jnp.logical_not(inner), entry >= DEEP))
                    def _():
                        at = entry - (amount - DEEP)
                        relay_copy(i, at, at).wait_recv()
                        share_copy(i, at).start()

                @pl.when(jnp.logical_not(inner))
                def _():
                    low, high = span_of(amount, index - 2 * LAG)

                    @pl.loop(jnp.minimum(low, 2 * DEEP - amount), jnp.minimum(high, 2 * DEEP - amount))
                    def _(place):
                        relay_copy(i, place, place).wait_recv()
                        share_copy(i, place).start()

    def kv_range(start, stop):
        bounds = sorted({start, stop, *(b for b in (slots, slots + WINDOW) if start < b < stop)})
        for low, high in zip(bounds, bounds[1:]):
            @pl.loop(low, high)
            def _(index):
                kv_sent((low - WINDOW) // slots, index - WINDOW)
                kv_start(low // slots, index)
                arrivals(index)

    def line_copies(stage, place, device):
        return [
            pltpu.make_async_remote_copy(
                src_ref=ref.at[here, place, core], dst_ref=ref.at[here, place, core],
                send_sem=line_send.at[i, stage], recv_sem=line_recv.at[i, stage],
                device_id=device, device_id_type=MESH,
            )
            for i, ref in enumerate((tokens, mixes))
        ]

    over_copies = line_copies(0, chip, across_device)
    mate_copies = line_copies(1, chip, mate_device)
    relay_copies = line_copies(2, across, mate_device)

    pair_copies = [
        pltpu.make_async_remote_copy(
            src_ref=ref.at[here, :, core], dst_ref=ref.at[here, :, core],
            send_sem=pair_send.at[i], recv_sem=pair_recv.at[i],
            device_id=pair, device_id_type=MESH,
        )
        for i, ref in enumerate((tokens, mixes))
    ]

    swap = pltpu.make_async_remote_copy(
        src_ref=folded.at[:, 1 - core], dst_ref=swapped,
        send_sem=swap_send, recv_sem=swap_recv,
        device_id=pair, device_id_type=MESH,
    )

    def plane_copies(step):
        other, device = in_plane(step)
        return [
            pltpu.make_async_remote_copy(
                src_ref=ref.at[here], dst_ref=ref.at[here],
                send_sem=plane_send.at[i, step], recv_sem=plane_recv.at[i, step],
                device_id=device, device_id_type=MESH,
            )
            for i, ref in enumerate((tokens, mixes))
        ]

    def part_copy(step):
        other, device = in_plane(step)
        return pltpu.make_async_remote_copy(
            src_ref=partial.at[other], dst_ref=gathered.at[step],
            send_sem=part_send.at[step], recv_sem=part_recv.at[step],
            device_id=device, device_id_type=MESH,
        )

    mate_swap = pltpu.make_async_remote_copy(
        src_ref=mate_out, dst_ref=mate_in, send_sem=mate_send, recv_sem=mate_recv,
        device_id=mate_device, device_id_type=MESH,
    )
    back = pltpu.make_async_remote_copy(
        src_ref=outgoing, dst_ref=returned, send_sem=back_send, recv_sem=back_recv,
        device_id=across_device, device_id_type=MESH,
    )

    for copy in over_copies + mate_copies:
        copy.start()

    @pl.when(g == 0)
    def _():
        for layer in lent_layers:
            lend_copy(layer).start()

    @pl.loop(0, WINDOW)
    def _(index):
        kv_start(0, index)

    marks = [WINDOW + (rounds - WINDOW) * i // 9 for i in range(10)]
    kv_range(marks[0], marks[1])

    for copy in over_copies:
        copy.wait()
    for copy in relay_copies:
        copy.start()
    kv_range(marks[1], marks[2])

    @pl.when(g == 1)
    def _():
        for layer in lent_layers:
            lend_copy(layer).wait_recv()
            for k in range(half_line):
                lent_copy(layer, k, seat).start()

    for copy in mate_copies + relay_copies:
        copy.wait()
    for copy in pair_copies:
        copy.start()
    kv_range(marks[2], marks[3])
    for copy in pair_copies:
        copy.wait()
    spread = [c for step in range(1, plane) for c in plane_copies(step)]
    for copy in spread:
        copy.start()

    kv_range(marks[3], marks[4])
    for copy in spread:
        copy.wait()

    expert = g * line + t
    width = tokens.shape[-1]
    count = line * rows

    @pl.loop(0, plane)
    def _(quarter):
        x = tokens[quarter].reshape(count, width)
        gate = jnp.dot(x, gate_w[0], preferred_element_type=jnp.float32)
        upper = jnp.dot(x, up_w[0], preferred_element_type=jnp.float32)
        active = (gate / (1.0 + jnp.exp(-gate)) * upper).astype(jnp.bfloat16)
        mixed = mixes[quarter].reshape(count, LANES)
        places = lax.broadcasted_iota(jnp.int32, (count, LANES), 1)
        weight = jnp.sum(jnp.where(places == expert, mixed, 0.0), axis=1, keepdims=True)
        out = jnp.dot(active, down_w[0], preferred_element_type=jnp.float32) * weight
        partial[quarter] = out.astype(jnp.bfloat16).reshape(chips, 2, rows, width)

    for step in range(1, plane):
        part_copy(step).start()
    kv_range(marks[4], marks[5])
    for step in range(1, plane):
        part_copy(step).wait()

    @pl.loop(0, chips)
    def _(place):
        for side in range(2):
            total = partial[here, place, side].astype(jnp.float32)
            for step in range(1, plane):
                total = total + gathered[step, place, side].astype(jnp.float32)
            folded[place, side] = total

    swap.start()
    kv_range(marks[5], marks[6])
    swap.wait()

    mate_out[0] = folded[mate, core] + swapped[mate]
    mate_out[1] = folded[mate_across, core] + swapped[mate_across]
    mate_swap.start()
    kv_range(marks[6], marks[7])
    mate_swap.wait()
    outgoing[...] = (folded[across, core] + swapped[across] + mate_in[1]).astype(jnp.bfloat16)
    back.start()
    kv_range(marks[7], marks[8])
    back.wait()
    total = folded[chip, core] + swapped[chip] + mate_in[0] + returned[...].astype(jnp.float32)
    moe_ref[...] = total.astype(jnp.bfloat16)

    kv_range(marks[8], marks[9])

    @pl.loop(rounds, rounds + 2 * LAG)
    def _(index):
        arrivals(index)

    @pl.loop(rounds - WINDOW, rounds)
    def _(index):
        kv_sent(layers - 1, index)

    @pl.when(g == 0)
    def _():
        for layer in range(layers):
            @pl.loop(layer * slots, (layer + 1) * slots)
            def _(index):
                for k in range(half_line):
                    far_copy(layer, index, k, k).wait_recv()
        for layer in lent_layers:
            lend_copy(layer).wait_send()
            for k in range(half_line):
                lent_copy(layer, k, k).wait_recv()

    @pl.loop(0, rounds)
    def _(index):
        for step in range(1, half_line):
            near_copy(index, step).wait_recv()

    @pl.when(g == 1)
    def _():
        for layer in lent_layers:
            for k in range(half_line):
                lent_copy(layer, k, seat).wait_send()

        @pl.loop(0, DEEP)
        def _(entry):
            for i in range(2):
                share_copy(i, entry).wait()

        @pl.when(inner)
        def _():
            for i in range(2):
                amount = cap_of(far_half * half_line + 2 * i + core)

                @pl.loop(amount - DEEP, DEEP)
                def _(entry):
                    relay_copy(i, entry, entry).wait_send()

    own.wait()


def units_of(length, start, block):
    return jnp.clip((length - start + UNIT - 1) // UNIT, 0, block // UNIT)


def pack_kernel(heads, lengths_ref, kv_ref, packed_ref, chosen_ref, sems):
    layers, slots_all, block, width = kv_ref.shape
    requests = slots_all // heads
    quarter = requests // 4
    g, t = lax.axis_index("group"), lax.axis_index("tensor")
    start = (g * LINE + t) * block
    far_half = jnp.where(t < LINE // 2, 1, 0)

    misses = [jnp.int32(0) for _ in PLANS]
    for device in range(LINE):
        first = requests // 2 if device < LINE // 2 else 0
        needed = jnp.int32(0)
        for number in range(first, first + requests // 2):
            needed = needed + units_of(lengths_ref[number], (LINE + device) * block, block)
        for i, plan in enumerate(PLANS):
            misses[i] = misses[i] + jnp.where(needed > plan[device], 1, 0)
    chosen = jnp.int32(len(PLANS) - 1)
    for i in reversed(range(len(PLANS) - 1)):
        chosen = jnp.where(misses[i] == 0, i, chosen)
    chosen_ref[0] = chosen
    cap = jnp.int32(0)
    for i, plan in enumerate(PLANS):
        mine = jnp.int32(0)
        for device in range(LINE):
            mine = mine + jnp.where(t == device, plan[device], 0)
        cap = cap + jnp.where(chosen == i, mine, 0)

    def each(act):
        for last in range(2):
            chip = 1 + far_half if last == 0 else 3 * far_half

            def request(r, before):
                number = chip * quarter + r
                amount = units_of(lengths_ref[number], start, block)

                @pl.loop(0, amount)
                def _(q):
                    k = before + q
                    entry = k if last == 0 else cap - 1 - k
                    act(number, q, entry)

                return before + amount

            lax.fori_loop(0, quarter, request, jnp.int32(0))

    def copy(number, q, entry):
        return pltpu.make_async_copy(
            kv_ref.at[:, pl.ds(number * heads, heads), pl.ds(pl.multiple_of(q * UNIT, UNIT), UNIT)],
            packed_ref.at[entry],
            sems.at[entry],
        )

    @pl.when(g == 1)
    def _():
        each(lambda *a: copy(*a).start())
        each(lambda *a: copy(*a).wait())


def pack(lengths, kv, heads):
    layers, slots_all, block, width = kv.shape
    in_smem = pl.BlockSpec(memory_space=pltpu.SMEM)
    return pl.pallas_call(
        functools.partial(pack_kernel, heads),
        out_shape=(
            pltpu.VMEM((2 * DEEP, layers, heads, UNIT, width), kv.dtype),
            jax.ShapeDtypeStruct((1,), jnp.int32),
        ),
        in_specs=[in_smem, pl.BlockSpec(memory_space=pl.ANY)],
        out_specs=(pl.BlockSpec(memory_space=pltpu.VMEM), in_smem),
        scratch_shapes=[pltpu.SemaphoreType.DMA((2 * DEEP,))],
        compiler_params=pltpu.CompilerParams(vmem_limit_bytes=1024 * 1024),
    )(lengths, kv)


def mask_kernel(
    heads, piece,
    lengths_ref, cache_ref, other_pool_ref, moe_ref,
    out_ref, moe_out_ref,
    zeros, zero_unit, edges, edge_units, sems, unit_sems, moe_sem,
):
    layers, slots, span, width = cache_ref.shape
    pieces = span // piece
    half_line = pieces // 2
    per_device = slots // heads
    per_block = piece // UNIT
    g, t = lax.axis_index("group"), lax.axis_index("tensor")
    base = g * span
    half, core, chip = t // half_line, lax.rem(t, 2), t // 2
    inner = jnp.logical_or(chip == 1, chip == 2)
    moe_copy = pltpu.make_async_copy(moe_ref, moe_out_ref, moe_sem)
    moe_copy.start()
    zeros[...] = jnp.zeros(zeros.shape, zeros.dtype)
    zero_unit[...] = jnp.zeros(zero_unit.shape, zero_unit.dtype)
    places = lax.broadcasted_iota(jnp.int32, (piece, width), 0)
    unit_places = lax.broadcasted_iota(jnp.int32, zero_unit.shape, 2)
    direct_low = jnp.where(g == 0, 0, half * half_line)
    direct_high = jnp.where(g == 0, pieces, half * half_line + half_line)

    def target(layer, slot, index):
        return out_ref.at[layer, slot, pl.ds(pl.multiple_of(index * piece, piece), piece)]

    def unit_target(r, source, q):
        start = pl.multiple_of(source * piece + q * UNIT, UNIT)
        return out_ref.at[:, pl.ds(r * heads, heads), pl.ds(start, UNIT)]

    @pl.loop(0, slots)
    def _(slot):
        length = lengths_ref[per_device * t + slot // heads] - base

        @pl.loop(direct_low, direct_high)
        def _(index):
            left = length - index * piece
            rows = pl.ds(pl.multiple_of(index * piece, piece), piece)
            for layer in range(layers):
                sem = sems.at[layer, slot, index]

                @pl.when(left >= piece)
                def _():
                    source = cache_ref.at[layer, slot, rows]
                    pltpu.make_async_copy(source, target(layer, slot, index), sem).start()

                @pl.when(left <= 0)
                def _():
                    pltpu.make_async_copy(zeros, target(layer, slot, index), sem).start()

                @pl.when(jnp.logical_and(left > 0, left < piece))
                def _():
                    edges[layer, slot] = jnp.where(
                        places < left, cache_ref[layer, slot, rows], jnp.zeros((), edges.dtype)
                    )
                    edge = edges.at[layer, slot]
                    pltpu.make_async_copy(edge, target(layer, slot, index), sem).start()

    @pl.when(g == 1)
    def _():
        @pl.loop(0, half_line)
        def _(k):
            source = (1 - half) * half_line + k
            start = base + source * piece
            before = jnp.int32(0)
            for r in range(2 * per_device):
                number = chip * 2 * per_device + r
                length = lengths_ref[number] - start
                mine = r - core * per_device

                @pl.when(jnp.logical_and(mine >= 0, mine < per_device))
                def _():
                    @pl.loop(0, per_block)
                    def _(q):
                        left = length - q * UNIT
                        order = before + q
                        entry = jnp.where(inner, order, DEEP - 1 - order)
                        rows = ((1 - half) * DEEP + entry) * UNIT
                        own_unit = cache_ref.at[
                            :, pl.ds((k // 2) * (slots // 2), slots // 2), pl.ds(pl.multiple_of(rows, UNIT), UNIT)
                        ]
                        at = unit_target(mine, source, q)
                        sem = unit_sems.at[mine, k, q]
                        for which, unit in enumerate((own_unit, other_pool_ref.at[k // 2, entry])):
                            here = (lax.rem(k, 2) == core) if which == 0 else (lax.rem(k, 2) != core)

                            @pl.when(jnp.logical_and(here, left >= UNIT))
                            def _():
                                pltpu.make_async_copy(unit, at, sem).start()

                            @pl.when(jnp.logical_and(here, jnp.logical_and(left > 0, left < UNIT)))
                            def _():
                                edge_units[mine] = jnp.where(
                                    unit_places < left, unit[...], jnp.zeros((), edges.dtype)
                                )
                                pltpu.make_async_copy(edge_units.at[mine], at, sem).start()

                        @pl.when(left <= 0)
                        def _():
                            pltpu.make_async_copy(zero_unit, at, sem).start()

                before = before + units_of(lengths_ref[number], start, piece)

    @pl.loop(0, slots)
    def _(slot):
        @pl.loop(direct_low, direct_high)
        def _(index):
            for layer in range(layers):
                sem = sems.at[layer, slot, index]
                pltpu.make_async_copy(zeros, target(layer, slot, index), sem).wait()

    @pl.when(g == 1)
    def _():
        @pl.loop(0, half_line)
        def _(k):
            source = (1 - half) * half_line + k
            for mine in range(per_device):
                @pl.loop(0, per_block)
                def _(q):
                    at = unit_target(mine, source, q)
                    pltpu.make_async_copy(zero_unit, at, unit_sems.at[mine, k, q]).wait()

    moe_copy.wait()


def mask_cache(lengths, cache, other_pool, moe, heads, piece):
    layers, slots, span, width = cache.shape
    in_smem = pl.BlockSpec(memory_space=pltpu.SMEM)
    in_vmem = pl.BlockSpec(memory_space=pltpu.VMEM)
    cache, other_pool, moe = (
        pltpu.with_memory_space_constraint(x, pltpu.VMEM) for x in (cache, other_pool, moe)
    )
    in_place = pl.BlockSpec(memory_space=pl.ANY)
    unit = (layers, heads, UNIT, width)
    pieces = span // piece
    return pl.pallas_call(
        functools.partial(mask_kernel, heads, piece),
        out_shape=(
            jax.ShapeDtypeStruct(cache.shape, cache.dtype),
            jax.ShapeDtypeStruct(moe.shape, moe.dtype),
        ),
        in_specs=[in_smem, in_vmem, in_vmem, in_vmem],
        out_specs=(in_place, in_place),
        scratch_shapes=[
            pltpu.VMEM((piece, width), cache.dtype),
            pltpu.VMEM(unit, cache.dtype),
            pltpu.VMEM((layers, slots, piece, width), cache.dtype),
            pltpu.VMEM((slots // heads, *unit), cache.dtype),
            pltpu.SemaphoreType.DMA((layers, slots, pieces)),
            pltpu.SemaphoreType.DMA((slots // heads, pieces // 2, piece // UNIT)),
            pltpu.SemaphoreType.DMA,
        ],
        compiler_params=pltpu.CompilerParams(vmem_limit_bytes=4 * 1024 * 1024),
    )(lengths, cache, other_pool, moe)


def fused_shards(
    sizes,
    hidden_states, norm_gain, expert_ids, route_weights, w_gate, w_up, w_down, prefill_key_value, lengths,
):
    groups, line, seqs = sizes
    plane, chips = groups * seqs, line // 2
    layers, requests, heads, block, width = prefill_key_value.shape
    rows, model_width = hidden_states.shape
    slots = requests * heads // line
    rounds = layers * slots
    bf16 = jnp.bfloat16
    dma = pltpu.SemaphoreType.DMA
    in_vmem = pl.BlockSpec(memory_space=pltpu.VMEM)
    in_hbm = pl.BlockSpec(memory_space=pl.ANY)
    kv = prefill_key_value.reshape(layers, requests * heads, block, width)

    packed, chosen = pack(lengths, kv, heads)
    pool_type = pltpu.VMEM((2, DEEP, *packed.shape[1:]), bf16)

    def branch(number):
        caps = PLANS[number]
        spare = 2 * DEEP * 4 - max(sum(caps[: line // 2]), sum(caps[line // 2 :]))
        cuts = (spare // 32 * 16, (spare + 16) // 32 * 16)

        def run(hidden_states, norm_gain, ids, weights, w_gate, w_up, w_down, kv, packed, lengths):
            moe_out, cache, other_pool = pl.pallas_call(
                functools.partial(fused_kernel, sizes, caps, cuts),
                out_shape=(
                    pltpu.VMEM((rows, model_width), bf16),
                    pltpu.VMEM((layers, slots, line * block, width), bf16),
                    pool_type,
                ),
                in_specs=[in_vmem] * 7 + [in_hbm, in_vmem],
                out_specs=(in_vmem,) * 3,
                scratch_shapes=[
                    pltpu.VMEM((plane, chips, 2, rows, model_width), bf16),
                    pltpu.VMEM((plane, chips, 2, rows, LANES), jnp.float32),
                    pltpu.VMEM((plane, chips, 2, rows, model_width), bf16),
                    pltpu.VMEM((plane, chips, 2, rows, model_width), bf16),
                    pltpu.VMEM((chips, 2, rows, model_width), jnp.float32),
                    pltpu.VMEM((chips, rows, model_width), jnp.float32),
                    pltpu.VMEM((2, rows, model_width), jnp.float32),
                    pltpu.VMEM((2, rows, model_width), jnp.float32),
                    pltpu.VMEM((rows, model_width), bf16),
                    pltpu.VMEM((rows, model_width), bf16),
                    pltpu.VMEM((line // 2 * slots, max(16, cuts[0]), width), bf16),
                    pltpu.VMEM((line // 2 * slots, max(16, cuts[1]), width), bf16),
                    dma((rounds, line // 2)),
                    dma((rounds, line // 2)),
                    dma((rounds, line // 2)),
                    dma((rounds, line // 2)),
                    dma,
                    dma((2 * DEEP,)),
                    dma((2, DEEP)),
                    dma((2, DEEP)),
                    dma((2, DEEP)),
                    dma((2, DEEP)),
                    dma((2,)),
                    dma((2,)),
                    dma((2, line // 2)),
                    dma((2, line // 2)),
                    dma((2, 3)),
                    dma((2, 3)),
                    dma((2,)),
                    dma((2,)),
                    dma((2, plane)),
                    dma((2, plane)),
                    dma((plane,)),
                    dma((plane,)),
                    dma,
                    dma,
                    dma,
                    dma,
                    dma,
                    dma,
                ],
                compiler_params=pltpu.CompilerParams(
                    collective_id=number, has_side_effects=True, vmem_limit_bytes=15 * 1024 * 1024
                ),
            )(hidden_states, norm_gain, ids, weights, w_gate, w_up, w_down, kv, packed)
            return mask_cache(lengths, cache, other_pool, moe_out, heads, block)

        return run

    cache, moe_out = lax.switch(
        chosen[0],
        [branch(number) for number in range(len(PLANS))],
        hidden_states, norm_gain, expert_ids.T, route_weights.T, w_gate, w_up, w_down, kv, packed, lengths,
    )
    return (moe_out, cache)


def solution(mesh):
    sizes = tuple(mesh.shape[name] for name in ("group", "tensor", "seq"))

    def shards(hidden_states, *rest):
        tokens = hidden_states.shape[0] * sizes[0] * sizes[1] * sizes[2]
        one_expert = rest[3].shape[0] == 1 and sizes[0] * sizes[1] <= LANES
        layers, requests, heads, block, width = rest[6].shape
        regular = layers == 2 and requests == 2 * LINE and heads * requests == 8 * LINE and block == 8 * UNIT
        if tokens <= DENSE_TOKENS and one_expert and sizes == (2, LINE, 2) and regular:
            return fused_shards(sizes, hidden_states, *rest)
        return routed_shards(hidden_states, *rest)

    return jax.shard_map(
        shards,
        mesh=mesh,
        in_specs=(
            P(("group", "tensor", "seq"), None),
            P(),
            P(("group", "tensor", "seq"), None),
            P(("group", "tensor", "seq"), None),
            P(("group", "tensor"), None, "seq"),
            P(("group", "tensor"), None, "seq"),
            P(("group", "tensor"), "seq", None),
            P("seq", None, None, ("group", "tensor"), None),
            P(),
        ),
        out_specs=(P(("group", "tensor", "seq"), None), P("seq", "tensor", "group", None)),
        check_vma=False,
    )
```

```python
import functools
import jax
import jax.numpy as jnp
from jax import lax
from jax.experimental import pallas as pl
from jax.experimental.pallas import tpu as pltpu
from jax.sharding import PartitionSpec as P

epsilon = 1e-06
LANES = 128
DENSE_TOKENS = 1024
WINDOW = 3
LINE = 8
RELAY_LAG = 3
SHARE_LAG = 4
LAST_LAG = 6
EASE = 16
UNIT = 32
DEEP = 32
PLANS = (
    (48, 48, 40, 40, 56, 48, 40, 32),
    (48, 48, 48, 48, 56, 56, 44, 32),
    (56, 48, 48, 40, 56, 56, 44, 32),
    (56, 56, 48, 48, 64, 56, 44, 32),
    (56, 56, 56, 56, 64, 60, 56, 44),
    (64, 64, 64, 64, 64, 64, 64, 64),
)
MESH = pl.DeviceIdType.MESH


def hand_over(prefill_key_value, lengths):
    layers_here, requests, heads, block, width = prefill_key_value.shape
    block_index = lax.axis_index("group") * lax.axis_size("tensor") + lax.axis_index("tensor")
    positions = block_index * block + jnp.arange(block, dtype=jnp.int32)
    keep = positions[None, :] < lengths[:, None]
    masked_entries = jnp.where(
        keep[None, :, None, :, None], prefill_key_value, jnp.zeros((), prefill_key_value.dtype)
    )
    flat = masked_entries.reshape(layers_here, requests * heads, block, width)
    return lax.all_to_all(flat, "tensor", split_axis=1, concat_axis=2, tiled=True)


def mixture(hidden_states, norm_gain, expert_ids, route_weights, w_gate, w_up, w_down):
    wide = hidden_states.astype(jnp.float32)
    scale = lax.rsqrt(jnp.mean(wide * wide, axis=1, keepdims=True) + epsilon)
    normed = (wide * scale * norm_gain.astype(jnp.float32)).astype(jnp.bfloat16)
    share = route_weights / jnp.sum(route_weights, axis=1, keepdims=True)
    expert_local, model_width, part_width = w_gate.shape
    sources = lax.axis_size("group") * lax.axis_size("tensor")
    experts = expert_local * sources
    rows_here, top_count = expert_ids.shape
    most = min(rows_here, max(2, 2 * rows_here * top_count // experts))
    flat_ids = expert_ids.reshape(-1)
    expert_grid = jnp.arange(experts, dtype=jnp.int32)
    onehot = (flat_ids[:, None] == expert_grid[None, :]).astype(jnp.int32)
    choices = jnp.arange(flat_ids.shape[0], dtype=jnp.int32)
    before = (choices[:, None] > choices[None, :]).astype(jnp.float32)
    earlier = jnp.dot(before, onehot.astype(jnp.float32), preferred_element_type=jnp.float32).astype(jnp.int32)
    position = jnp.sum(earlier * onehot, axis=1)
    target = flat_ids * most + position
    slot_grid = jnp.arange(experts * most, dtype=jnp.int32)
    hits = (target[:, None] == slot_grid[None, :]).reshape(rows_here, top_count, experts * most)
    select = jnp.sum(hits.astype(jnp.float32), axis=1).astype(jnp.bfloat16)
    mixing = jnp.sum(jnp.where(hits, share[:, :, None], 0.0), axis=1)
    outgoing = lax.dot_general(
        select, normed, (((0,), (0,)), ((), ())), preferred_element_type=jnp.float32
    )
    outgoing = outgoing.astype(jnp.bfloat16).reshape(experts, most, model_width)
    arrived = lax.all_to_all(outgoing, ("group", "tensor"), split_axis=0, concat_axis=0, tiled=True)
    arrived = arrived.reshape(sources, expert_local, most, model_width)
    pooled = lax.all_gather(arrived, "seq", axis=0, tiled=True)
    gate = jnp.einsum("semd,edf->semf", pooled, w_gate, preferred_element_type=jnp.float32)
    upper = jnp.einsum("semd,edf->semf", pooled, w_up, preferred_element_type=jnp.float32)
    active = (jax.nn.silu(gate) * upper).astype(jnp.bfloat16)
    summed = lax.psum_scatter(
        jnp.einsum("semf,efd->semd", active, w_down, preferred_element_type=jnp.float32).astype(
            jnp.bfloat16
        ),
        "seq",
        scatter_dimension=0,
        tiled=True,
    )
    returned = lax.all_to_all(
        summed.reshape(sources * expert_local, most, model_width),
        ("group", "tensor"),
        split_axis=0,
        concat_axis=0,
        tiled=True,
    )
    flat_back = returned.reshape(experts * most, model_width).astype(jnp.float32)
    mixed = jnp.dot(mixing, flat_back, precision=lax.Precision.HIGHEST)
    return mixed.astype(jnp.bfloat16)


def routed_shards(
    hidden_states, norm_gain, expert_ids, route_weights, w_gate, w_up, w_down, prefill_key_value, lengths
):
    moe_out = mixture(hidden_states, norm_gain, expert_ids, route_weights, w_gate, w_up, w_down)
    decoder_slot_cache = hand_over(prefill_key_value, lengths)
    return (moe_out, decoder_slot_cache)


def fused_kernel(
    sizes, caps, cuts,
    hidden_ref, gain_ref, ids_ref, weights_ref, gate_w, up_w, down_w, kv_ref, packed_ref,
    moe_ref, cache_ref, other_pool_ref,
    tokens, mixes, partial, gathered, folded, swapped, mate_out, mate_in, outgoing, returned,
    lend_first, lend_last,
    near_send, near_recv, far_send, far_recv, own_sem,
    stream_send, stream_recv, relay_send, share_send, share_recv, lend_send, lend_recv, lent_send, lent_recv,
    line_send, line_recv, pair_send, pair_recv, plane_send, plane_recv,
    part_send, part_recv, swap_send, swap_recv, mate_send, mate_recv, back_send, back_recv,
):
    groups, line, seqs = sizes
    plane = groups * seqs
    g, t, s = lax.axis_index("group"), lax.axis_index("tensor"), lax.axis_index("seq")
    here = g * seqs + s
    chips = line // 2
    chip, core = t // 2, lax.rem(t, 2)
    pair = (g, t + 1 - 2 * core, s)
    mate = chip + 1 - 2 * lax.rem(chip, 2)
    across, mate_across = lax.rem(chip + 2, chips), lax.rem(mate + 2, chips)
    mate_device, across_device = (g, mate * 2 + core, s), (g, across * 2 + core, s)
    layers, slots_all, block, _ = kv_ref.shape
    slots = slots_all // line
    rounds = layers * slots
    half_line = line // 2
    half, seat = t // half_line, lax.rem(t, half_line)
    far_half = 1 - half

    def in_line(step):
        other = lax.rem(t + step, line)
        return other, (g, other, s)

    def in_plane(step):
        other = lax.rem(here + step, plane)
        return other, (other // seqs, t, lax.rem(other, seqs))

    barrier = pltpu.get_barrier_semaphore()
    for step in range(1, line):
        pl.semaphore_signal(barrier, inc=1, device_id=in_line(step)[1], device_id_type=MESH)
    for step in range(1, plane):
        pl.semaphore_signal(barrier, inc=1, device_id=in_plane(step)[1], device_id_type=MESH)
    for k in range(half_line):
        pl.semaphore_signal(
            barrier, inc=1, device_id=(1 - g, far_half * half_line + k, s), device_id_type=MESH
        )

    columns = pl.ds(pl.multiple_of(t * block, block), block)
    own = pltpu.make_async_copy(
        kv_ref.at[:, pl.ds(t * slots, slots)], cache_ref.at[:, :, columns], own_sem
    )
    own.start()

    wide = hidden_ref[...].astype(jnp.float32)
    scale = lax.rsqrt(jnp.mean(wide * wide, axis=1, keepdims=True) + epsilon)
    tokens[here, chip, core] = (wide * scale * gain_ref[...].astype(jnp.float32)[None, :]).astype(jnp.bfloat16)
    top, rows = ids_ref.shape
    ids = ids_ref[...].T
    weights = weights_ref[...].T
    share = weights / jnp.sum(weights, axis=1, keepdims=True)
    lane = lax.broadcasted_iota(jnp.int32, (rows, LANES), 1)
    mix = jnp.zeros((rows, LANES), jnp.float32)
    for k in range(top):
        mix = mix + jnp.where(lane == ids[:, k : k + 1], share[:, k : k + 1], 0.0)
    mixes[here, chip, core] = mix

    pl.semaphore_wait(barrier, line + plane - 2 + half_line)

    def cap_of(device):
        total = 0
        for k in range(line):
            total = total + jnp.where(device == k, caps[k], 0)
        return total

    cap = cap_of(t)
    inner = jnp.logical_or(chip == 1, chip == 2)
    first_chip, last_chip = 1 + far_half * 1, far_half * 3
    lane_index = lax.rem(chip, 2)

    def pool(side, lane, entry):
        start = pl.multiple_of((side * DEEP + entry) * UNIT, UNIT)
        return cache_ref.at[:, pl.ds(lane * (slots // 2), slots // 2), pl.ds(start, UNIT)]

    def near_copy(index, step):
        other = half * half_line + lax.rem(seat + step, half_line)
        layer, slot = index // slots, lax.rem(index, slots)
        return pltpu.make_async_remote_copy(
            src_ref=kv_ref.at[layer, other * slots + slot],
            dst_ref=cache_ref.at[layer, slot, columns],
            send_sem=near_send.at[index, step],
            recv_sem=near_recv.at[index, step],
            device_id=(g, other, s),
            device_id_type=MESH,
        )

    def far_copy(layer, index, k, source):
        other = far_half * half_line + k
        at, slot = index // slots, lax.rem(index, slots)
        kept = block - cuts[layer]
        return pltpu.make_async_remote_copy(
            src_ref=kv_ref.at[at, other * slots + slot, pl.ds(0, kept)],
            dst_ref=cache_ref.at[at, slot, pl.ds(pl.multiple_of(t * block, block), kept)],
            send_sem=far_send.at[index, k],
            recv_sem=far_recv.at[index, source],
            device_id=(g, other, s),
            device_id_type=MESH,
        )

    def both_before(place, amount):
        return jnp.minimum(place, 2 * DEEP - amount)

    def entry_at(place, amount):
        rest = place - (2 * DEEP - amount)
        single = amount - DEEP
        swapped_turns = jnp.where(lax.rem(rest, 2) == 0, DEEP + rest // 2, rest // 2)
        in_order = jnp.where(rest < single, DEEP + rest, rest - single)
        one = jnp.where(amount == 2 * DEEP, swapped_turns, in_order)
        return jnp.where(rest < 0, place + single, one)

    def stream_copy(place):
        entry = entry_at(place, cap)
        first = entry < DEEP
        target = jnp.where(first, entry, entry - (cap - DEEP))
        return pltpu.make_async_remote_copy(
            src_ref=packed_ref.at[entry],
            dst_ref=pool(half, lane_index, target),
            send_sem=stream_send.at[entry],
            recv_sem=stream_recv.at[lane_index, target],
            device_id=(g, jnp.where(first, first_chip, last_chip) * 2 + core, s),
            device_id_type=MESH,
        )

    def share_copy(lane, entry):
        return pltpu.make_async_remote_copy(
            src_ref=pool(far_half, lane, entry), dst_ref=other_pool_ref.at[lane, entry],
            send_sem=share_send.at[lane, entry], recv_sem=share_recv.at[lane, entry],
            device_id=pair, device_id_type=MESH,
        )

    def relay_copy(lane, entry, target):
        return pltpu.make_async_remote_copy(
            src_ref=pool(far_half, lane, entry), dst_ref=pool(far_half, lane, target),
            send_sem=relay_send.at[lane, entry], recv_sem=stream_recv.at[lane, target],
            device_id=mate_device, device_id_type=MESH,
        )

    def span_of(amount, index):
        at = jnp.clip(index, 0, rounds)
        after = jnp.clip(index + 1, 0, rounds)
        return amount * at // rounds, amount * after // rounds

    lends = [buffer for buffer in (lend_first, lend_last)]

    def lend_copy(layer):
        cut = cuts[layer]
        return pltpu.make_async_remote_copy(
            src_ref=kv_ref.at[layer, pl.ds(far_half * half_line * slots, half_line * slots), pl.ds(block - cut, cut)],
            dst_ref=lends[layer],
            send_sem=lend_send.at[layer], recv_sem=lend_recv.at[layer],
            device_id=(1 - g, t, s), device_id_type=MESH,
        )

    def lent_copy(layer, k, source):
        cut = cuts[layer]
        start = pl.multiple_of(t * block + block - cut, 16)
        return pltpu.make_async_remote_copy(
            src_ref=lends[layer].at[pl.ds(k * slots, slots)],
            dst_ref=cache_ref.at[layer, :, pl.ds(start, cut)],
            send_sem=lent_send.at[layer, k], recv_sem=lent_recv.at[layer, source],
            device_id=(1 - g, far_half * half_line + k, s), device_id_type=MESH,
        )

    lent_layers = [layer for layer in range(layers) if cuts[layer] > 0]

    def far_each(index, source, act):
        if cuts[0] == cuts[1]:
            for k in range(half_line):
                act(far_copy(0, index, k, k if source is None else source))
            return
        for layer in range(layers):
            @pl.when(index // slots == layer)
            def _():
                for k in range(half_line):
                    act(far_copy(layer, index, k, k if source is None else source))

    def kv_start(index):
        for step in range(1, half_line):
            near_copy(index, step).start()

        @pl.when(g == 0)
        def _():
            far_each(index, seat, lambda copy: copy.start())

        @pl.when(g == 1)
        def _():
            @pl.loop(*span_of(cap, index))
            def _(place):
                stream_copy(place).start()

    def kv_sent(index):
        for step in range(1, half_line):
            near_copy(index, step).wait_send()

        @pl.when(g == 0)
        def _():
            far_each(index, seat, lambda copy: copy.wait_send())

        @pl.when(g == 1)
        def _():
            @pl.loop(*span_of(cap, index))
            def _(place):
                stream_copy(place).wait_send()

    def arrivals(index):
        @pl.when(g == 1)
        def _():
            for i in range(2):
                amount = cap_of(far_half * half_line + 2 * i + core)

                @pl.when(inner)
                def _():
                    low, high = span_of(amount, index - RELAY_LAG)

                    @pl.loop(both_before(low, amount), both_before(high, amount))
                    def _(place):
                        relay_copy(i, place + amount - DEEP, place + amount - DEEP).wait_recv()
                        relay_copy(i, place + amount - DEEP, place).start()

                @pl.loop(*span_of(amount, index - SHARE_LAG))
                def _(place):
                    entry = entry_at(place, amount)

                    @pl.when(jnp.logical_and(inner, entry < DEEP))
                    def _():
                        @pl.when(entry < amount - DEEP)
                        def _():
                            relay_copy(i, entry, entry).wait_recv()

                        share_copy(i, entry).start()

                    @pl.when(jnp.logical_and(jnp.logical_not(inner), entry >= DEEP))
                    def _():
                        at = entry - (amount - DEEP)
                        relay_copy(i, at, at).wait_recv()
                        share_copy(i, at).start()

                @pl.when(jnp.logical_not(inner))
                def _():
                    low, high = span_of(amount, index - LAST_LAG)

                    @pl.loop(both_before(low, amount), both_before(high, amount))
                    def _(place):
                        relay_copy(i, place, place).wait_recv()
                        share_copy(i, place).start()

    def line_copies(stage, place, device):
        return [
            pltpu.make_async_remote_copy(
                src_ref=ref.at[here, place, core], dst_ref=ref.at[here, place, core],
                send_sem=line_send.at[i, stage], recv_sem=line_recv.at[i, stage],
                device_id=device, device_id_type=MESH,
            )
            for i, ref in enumerate((tokens, mixes))
        ]

    over_copies = line_copies(0, chip, across_device)
    mate_copies = line_copies(1, chip, mate_device)
    relay_copies = line_copies(2, across, mate_device)

    pair_copies = [
        pltpu.make_async_remote_copy(
            src_ref=ref.at[here, :, core], dst_ref=ref.at[here, :, core],
            send_sem=pair_send.at[i], recv_sem=pair_recv.at[i],
            device_id=pair, device_id_type=MESH,
        )
        for i, ref in enumerate((tokens, mixes))
    ]

    swap = pltpu.make_async_remote_copy(
        src_ref=folded.at[:, 1 - core], dst_ref=swapped,
        send_sem=swap_send, recv_sem=swap_recv,
        device_id=pair, device_id_type=MESH,
    )

    def plane_copies(step):
        other, device = in_plane(step)
        return [
            pltpu.make_async_remote_copy(
                src_ref=ref.at[here], dst_ref=ref.at[here],
                send_sem=plane_send.at[i, step], recv_sem=plane_recv.at[i, step],
                device_id=device, device_id_type=MESH,
            )
            for i, ref in enumerate((tokens, mixes))
        ]

    def part_copy(step):
        other, device = in_plane(step)
        return pltpu.make_async_remote_copy(
            src_ref=partial.at[other], dst_ref=gathered.at[step],
            send_sem=part_send.at[step], recv_sem=part_recv.at[step],
            device_id=device, device_id_type=MESH,
        )

    mate_swap = pltpu.make_async_remote_copy(
        src_ref=mate_out, dst_ref=mate_in, send_sem=mate_send, recv_sem=mate_recv,
        device_id=mate_device, device_id_type=MESH,
    )
    back = pltpu.make_async_remote_copy(
        src_ref=outgoing, dst_ref=returned, send_sem=back_send, recv_sem=back_recv,
        device_id=across_device, device_id_type=MESH,
    )

    for copy in over_copies + mate_copies:
        copy.start()

    @pl.when(g == 0)
    def _():
        for layer in lent_layers:
            lend_copy(layer).start()

    spread = [c for step in range(1, plane) for c in plane_copies(step)]
    expert = g * line + t
    width = tokens.shape[-1]
    count = line * rows

    def across_done():
        for copy in over_copies:
            copy.wait()
        for copy in relay_copies:
            copy.start()

    def line_done():
        @pl.when(g == 1)
        def _():
            for layer in lent_layers:
                lend_copy(layer).wait_recv()
                for k in range(half_line):
                    lent_copy(layer, k, seat).start()

        for copy in mate_copies + relay_copies:
            copy.wait()
        for copy in pair_copies:
            copy.start()

    def pair_done():
        for copy in pair_copies:
            copy.wait()
        for copy in spread:
            copy.start()

    def spread_done():
        for copy in spread:
            copy.wait()

        @pl.loop(0, plane)
        def _(quarter):
            x = tokens[quarter].reshape(count, width)
            gate = jnp.dot(x, gate_w[0], preferred_element_type=jnp.float32)
            upper = jnp.dot(x, up_w[0], preferred_element_type=jnp.float32)
            active = (gate / (1.0 + jnp.exp(-gate)) * upper).astype(jnp.bfloat16)
            mixed = mixes[quarter].reshape(count, LANES)
            places = lax.broadcasted_iota(jnp.int32, (count, LANES), 1)
            weight = jnp.sum(jnp.where(places == expert, mixed, 0.0), axis=1, keepdims=True)
            out = jnp.dot(active, down_w[0], preferred_element_type=jnp.float32) * weight
            partial[quarter] = out.astype(jnp.bfloat16).reshape(chips, 2, rows, width)

        for step in range(1, plane):
            part_copy(step).start()

    def parts_done():
        for step in range(1, plane):
            part_copy(step).wait()

        @pl.loop(0, chips)
        def _(place):
            for side in range(2):
                total = partial[here, place, side].astype(jnp.float32)
                for step in range(1, plane):
                    total = total + gathered[step, place, side].astype(jnp.float32)
                folded[place, side] = total

        swap.start()

    def swap_done():
        swap.wait()
        mate_out[0] = folded[mate, core] + swapped[mate]
        mate_out[1] = folded[mate_across, core] + swapped[mate_across]
        mate_swap.start()

    def mate_done():
        mate_swap.wait()
        outgoing[...] = (folded[across, core] + swapped[across] + mate_in[1]).astype(jnp.bfloat16)
        back.start()

    def back_done():
        back.wait()
        total = folded[chip, core] + swapped[chip] + mate_in[0] + returned[...].astype(jnp.float32)
        moe_ref[...] = total.astype(jnp.bfloat16)

    stages = (across_done, line_done, pair_done, spread_done, parts_done, swap_done, mate_done, back_done)

    @pl.loop(0, rounds + LAST_LAG)
    def _(index):
        for i, stage in enumerate(stages):
            pl.when(index == WINDOW + (rounds - WINDOW) * (i + 1) // 9)(stage)

        @pl.when(jnp.logical_and(index >= WINDOW, index < rounds))
        def _():
            kv_sent(index - WINDOW)

        @pl.when(index < rounds)
        def _():
            kv_start(index)

        arrivals(index)

    @pl.loop(rounds - WINDOW, rounds)
    def _(index):
        kv_sent(index)

    @pl.when(g == 0)
    def _():
        @pl.loop(0, rounds)
        def _(index):
            far_each(index, None, lambda copy: copy.wait_recv())

        for layer in lent_layers:
            lend_copy(layer).wait_send()
            for k in range(half_line):
                lent_copy(layer, k, k).wait_recv()

    @pl.loop(0, rounds)
    def _(index):
        for step in range(1, half_line):
            near_copy(index, step).wait_recv()

    @pl.when(g == 1)
    def _():
        for layer in lent_layers:
            for k in range(half_line):
                lent_copy(layer, k, seat).wait_send()

        @pl.loop(0, DEEP)
        def _(entry):
            for i in range(2):
                share_copy(i, entry).wait()

        @pl.when(inner)
        def _():
            for i in range(2):
                amount = cap_of(far_half * half_line + 2 * i + core)

                @pl.loop(amount - DEEP, DEEP)
                def _(entry):
                    relay_copy(i, entry, entry).wait_send()

    own.wait()


def units_of(length, start, block):
    return jnp.clip((length - start + UNIT - 1) // UNIT, 0, block // UNIT)


def pack_kernel(heads, lengths_ref, kv_ref, packed_ref, chosen_ref, sems):
    layers, slots_all, block, width = kv_ref.shape
    requests = slots_all // heads
    quarter = requests // 4
    g, t = lax.axis_index("group"), lax.axis_index("tensor")
    start = (g * LINE + t) * block
    far_half = jnp.where(t < LINE // 2, 1, 0)

    misses = [jnp.int32(0) for _ in PLANS]
    for device in range(LINE):
        first = requests // 2 if device < LINE // 2 else 0
        needed = jnp.int32(0)
        for number in range(first, first + requests // 2):
            needed = needed + units_of(lengths_ref[number], (LINE + device) * block, block)
        for i, plan in enumerate(PLANS):
            misses[i] = misses[i] + jnp.where(needed > plan[device], 1, 0)
    chosen = jnp.int32(len(PLANS) - 1)
    for i in reversed(range(len(PLANS) - 1)):
        chosen = jnp.where(misses[i] == 0, i, chosen)
    chosen_ref[0] = chosen
    cap = jnp.int32(0)
    for i, plan in enumerate(PLANS):
        mine = jnp.int32(0)
        for device in range(LINE):
            mine = mine + jnp.where(t == device, plan[device], 0)
        cap = cap + jnp.where(chosen == i, mine, 0)

    def each(act):
        for last in range(2):
            chip = 1 + far_half if last == 0 else 3 * far_half

            def request(r, before):
                number = chip * quarter + r
                amount = units_of(lengths_ref[number], start, block)

                @pl.loop(0, amount)
                def _(q):
                    k = before + q
                    entry = k if last == 0 else cap - 1 - k
                    act(number, q, entry)

                return before + amount

            lax.fori_loop(0, quarter, request, jnp.int32(0))

    def copy(number, q, entry):
        return pltpu.make_async_copy(
            kv_ref.at[:, pl.ds(number * heads, heads), pl.ds(pl.multiple_of(q * UNIT, UNIT), UNIT)],
            packed_ref.at[entry],
            sems.at[entry],
        )

    @pl.when(g == 1)
    def _():
        each(lambda *a: copy(*a).start())
        each(lambda *a: copy(*a).wait())


def pack(lengths, kv, heads):
    layers, slots_all, block, width = kv.shape
    in_smem = pl.BlockSpec(memory_space=pltpu.SMEM)
    return pl.pallas_call(
        functools.partial(pack_kernel, heads),
        out_shape=(
            pltpu.VMEM((2 * DEEP, layers, heads, UNIT, width), kv.dtype),
            jax.ShapeDtypeStruct((1,), jnp.int32),
        ),
        in_specs=[in_smem, pl.BlockSpec(memory_space=pl.ANY)],
        out_specs=(pl.BlockSpec(memory_space=pltpu.VMEM), in_smem),
        scratch_shapes=[pltpu.SemaphoreType.DMA((2 * DEEP,))],
        compiler_params=pltpu.CompilerParams(vmem_limit_bytes=1024 * 1024),
    )(lengths, kv)


def mask_kernel(
    heads, piece,
    lengths_ref, cache_ref, other_pool_ref, moe_ref,
    out_ref, moe_out_ref,
    zeros, zero_unit, edges, edge_units, sems, unit_sems, moe_sem,
):
    layers, slots, span, width = cache_ref.shape
    pieces = span // piece
    half_line = pieces // 2
    per_device = slots // heads
    per_block = piece // UNIT
    g, t = lax.axis_index("group"), lax.axis_index("tensor")
    base = g * span
    half, core, chip = t // half_line, lax.rem(t, 2), t // 2
    inner = jnp.logical_or(chip == 1, chip == 2)
    moe_copy = pltpu.make_async_copy(moe_ref, moe_out_ref, moe_sem)
    moe_copy.start()
    zeros[...] = jnp.zeros(zeros.shape, zeros.dtype)
    zero_unit[...] = jnp.zeros(zero_unit.shape, zero_unit.dtype)
    places = lax.broadcasted_iota(jnp.int32, (piece, width), 0)
    unit_places = lax.broadcasted_iota(jnp.int32, zero_unit.shape, 2)
    direct_low = jnp.where(g == 0, 0, half * half_line)
    direct_high = jnp.where(g == 0, pieces, half * half_line + half_line)

    def target(layer, slot, index):
        return out_ref.at[layer, slot, pl.ds(pl.multiple_of(index * piece, piece), piece)]

    def unit_target(r, source, q):
        start = pl.multiple_of(source * piece + q * UNIT, UNIT)
        return out_ref.at[:, pl.ds(r * heads, heads), pl.ds(start, UNIT)]

    @pl.loop(0, slots)
    def _(slot):
        length = lengths_ref[per_device * t + slot // heads] - base

        @pl.loop(direct_low, direct_high)
        def _(index):
            left = length - index * piece
            rows = pl.ds(pl.multiple_of(index * piece, piece), piece)
            for layer in range(layers):
                sem = sems.at[layer, slot, index]

                @pl.when(left >= piece)
                def _():
                    source = cache_ref.at[layer, slot, rows]
                    pltpu.make_async_copy(source, target(layer, slot, index), sem).start()

                @pl.when(left <= 0)
                def _():
                    pltpu.make_async_copy(zeros, target(layer, slot, index), sem).start()

                @pl.when(jnp.logical_and(left > 0, left < piece))
                def _():
                    edges[layer, slot] = jnp.where(
                        places < left, cache_ref[layer, slot, rows], jnp.zeros((), edges.dtype)
                    )
                    edge = edges.at[layer, slot]
                    pltpu.make_async_copy(edge, target(layer, slot, index), sem).start()

    @pl.when(g == 1)
    def _():
        @pl.loop(0, half_line)
        def _(k):
            source = (1 - half) * half_line + k
            start = base + source * piece
            before = jnp.int32(0)
            for r in range(2 * per_device):
                number = chip * 2 * per_device + r
                length = lengths_ref[number] - start
                mine = r - core * per_device

                @pl.when(jnp.logical_and(mine >= 0, mine < per_device))
                def _():
                    @pl.loop(0, per_block)
                    def _(q):
                        left = length - q * UNIT
                        order = before + q
                        entry = jnp.where(inner, order, DEEP - 1 - order)
                        rows = ((1 - half) * DEEP + entry) * UNIT
                        own_unit = cache_ref.at[
                            :, pl.ds((k // 2) * (slots // 2), slots // 2), pl.ds(pl.multiple_of(rows, UNIT), UNIT)
                        ]
                        at = unit_target(mine, source, q)
                        sem = unit_sems.at[mine, k, q]
                        for which, unit in enumerate((own_unit, other_pool_ref.at[k // 2, entry])):
                            here = (lax.rem(k, 2) == core) if which == 0 else (lax.rem(k, 2) != core)

                            @pl.when(jnp.logical_and(here, left >= UNIT))
                            def _():
                                pltpu.make_async_copy(unit, at, sem).start()

                            @pl.when(jnp.logical_and(here, jnp.logical_and(left > 0, left < UNIT)))
                            def _():
                                edge_units[mine] = jnp.where(
                                    unit_places < left, unit[...], jnp.zeros((), edges.dtype)
                                )
                                pltpu.make_async_copy(edge_units.at[mine], at, sem).start()

                        @pl.when(left <= 0)
                        def _():
                            pltpu.make_async_copy(zero_unit, at, sem).start()

                before = before + units_of(lengths_ref[number], start, piece)

    @pl.loop(0, slots)
    def _(slot):
        @pl.loop(direct_low, direct_high)
        def _(index):
            for layer in range(layers):
                sem = sems.at[layer, slot, index]
                pltpu.make_async_copy(zeros, target(layer, slot, index), sem).wait()

    @pl.when(g == 1)
    def _():
        @pl.loop(0, half_line)
        def _(k):
            source = (1 - half) * half_line + k
            for mine in range(per_device):
                @pl.loop(0, per_block)
                def _(q):
                    at = unit_target(mine, source, q)
                    pltpu.make_async_copy(zero_unit, at, unit_sems.at[mine, k, q]).wait()

    moe_copy.wait()


def mask_cache(lengths, cache, other_pool, moe, heads, piece):
    layers, slots, span, width = cache.shape
    in_smem = pl.BlockSpec(memory_space=pltpu.SMEM)
    in_vmem = pl.BlockSpec(memory_space=pltpu.VMEM)
    cache, other_pool, moe = (
        pltpu.with_memory_space_constraint(x, pltpu.VMEM) for x in (cache, other_pool, moe)
    )
    in_place = pl.BlockSpec(memory_space=pl.ANY)
    unit = (layers, heads, UNIT, width)
    pieces = span // piece
    return pl.pallas_call(
        functools.partial(mask_kernel, heads, piece),
        out_shape=(
            jax.ShapeDtypeStruct(cache.shape, cache.dtype),
            jax.ShapeDtypeStruct(moe.shape, moe.dtype),
        ),
        in_specs=[in_smem, in_vmem, in_vmem, in_vmem],
        out_specs=(in_place, in_place),
        scratch_shapes=[
            pltpu.VMEM((piece, width), cache.dtype),
            pltpu.VMEM(unit, cache.dtype),
            pltpu.VMEM((layers, slots, piece, width), cache.dtype),
            pltpu.VMEM((slots // heads, *unit), cache.dtype),
            pltpu.SemaphoreType.DMA((layers, slots, pieces)),
            pltpu.SemaphoreType.DMA((slots // heads, pieces // 2, piece // UNIT)),
            pltpu.SemaphoreType.DMA,
        ],
        compiler_params=pltpu.CompilerParams(vmem_limit_bytes=4 * 1024 * 1024),
    )(lengths, cache, other_pool, moe)


def fused_shards(
    sizes,
    hidden_states, norm_gain, expert_ids, route_weights, w_gate, w_up, w_down, prefill_key_value, lengths,
):
    groups, line, seqs = sizes
    plane, chips = groups * seqs, line // 2
    layers, requests, heads, block, width = prefill_key_value.shape
    rows, model_width = hidden_states.shape
    slots = requests * heads // line
    rounds = layers * slots
    bf16 = jnp.bfloat16
    dma = pltpu.SemaphoreType.DMA
    in_vmem = pl.BlockSpec(memory_space=pltpu.VMEM)
    in_hbm = pl.BlockSpec(memory_space=pl.ANY)
    kv = prefill_key_value.reshape(layers, requests * heads, block, width)

    packed, chosen = pack(lengths, kv, heads)
    pool_type = pltpu.VMEM((2, DEEP, *packed.shape[1:]), bf16)

    def branch(number):
        caps = PLANS[number]
        spare = 2 * DEEP * 4 - max(sum(caps[: line // 2]), sum(caps[line // 2 :]))
        spare = spare - EASE if spare >= 4 * EASE else spare
        cuts = (spare // 32 * 16, (spare + 16) // 32 * 16)

        def run(hidden_states, norm_gain, ids, weights, w_gate, w_up, w_down, kv, packed, lengths):
            moe_out, cache, other_pool = pl.pallas_call(
                functools.partial(fused_kernel, sizes, caps, cuts),
                out_shape=(
                    pltpu.VMEM((rows, model_width), bf16),
                    pltpu.VMEM((layers, slots, line * block, width), bf16),
                    pool_type,
                ),
                in_specs=[in_vmem] * 7 + [in_hbm, in_vmem],
                out_specs=(in_vmem,) * 3,
                scratch_shapes=[
                    pltpu.VMEM((plane, chips, 2, rows, model_width), bf16),
                    pltpu.VMEM((plane, chips, 2, rows, LANES), jnp.float32),
                    pltpu.VMEM((plane, chips, 2, rows, model_width), bf16),
                    pltpu.VMEM((plane, chips, 2, rows, model_width), bf16),
                    pltpu.VMEM((chips, 2, rows, model_width), jnp.float32),
                    pltpu.VMEM((chips, rows, model_width), jnp.float32),
                    pltpu.VMEM((2, rows, model_width), jnp.float32),
                    pltpu.VMEM((2, rows, model_width), jnp.float32),
                    pltpu.VMEM((rows, model_width), bf16),
                    pltpu.VMEM((rows, model_width), bf16),
                    pltpu.VMEM((line // 2 * slots, max(16, cuts[0]), width), bf16),
                    pltpu.VMEM((line // 2 * slots, max(16, cuts[1]), width), bf16),
                    dma((rounds, line // 2)),
                    dma((rounds, line // 2)),
                    dma((rounds, line // 2)),
                    dma((rounds, line // 2)),
                    dma,
                    dma((2 * DEEP,)),
                    dma((2, DEEP)),
                    dma((2, DEEP)),
                    dma((2, DEEP)),
                    dma((2, DEEP)),
                    dma((2,)),
                    dma((2,)),
                    dma((2, line // 2)),
                    dma((2, line // 2)),
                    dma((2, 3)),
                    dma((2, 3)),
                    dma((2,)),
                    dma((2,)),
                    dma((2, plane)),
                    dma((2, plane)),
                    dma((plane,)),
                    dma((plane,)),
                    dma,
                    dma,
                    dma,
                    dma,
                    dma,
                    dma,
                ],
                compiler_params=pltpu.CompilerParams(
                    collective_id=number, has_side_effects=True, vmem_limit_bytes=15 * 1024 * 1024
                ),
            )(hidden_states, norm_gain, ids, weights, w_gate, w_up, w_down, kv, packed)
            return mask_cache(lengths, cache, other_pool, moe_out, heads, block)

        return run

    cache, moe_out = lax.switch(
        chosen[0],
        [branch(number) for number in range(len(PLANS))],
        hidden_states, norm_gain, expert_ids.T, route_weights.T, w_gate, w_up, w_down, kv, packed, lengths,
    )
    return (moe_out, cache)


def solution(mesh):
    sizes = tuple(mesh.shape[name] for name in ("group", "tensor", "seq"))

    def shards(hidden_states, *rest):
        tokens = hidden_states.shape[0] * sizes[0] * sizes[1] * sizes[2]
        one_expert = rest[3].shape[0] == 1 and sizes[0] * sizes[1] <= LANES
        layers, requests, heads, block, width = rest[6].shape
        regular = layers == 2 and requests == 2 * LINE and heads * requests == 8 * LINE and block == 8 * UNIT
        if tokens <= DENSE_TOKENS and one_expert and sizes == (2, LINE, 2) and regular:
            return fused_shards(sizes, hidden_states, *rest)
        return routed_shards(hidden_states, *rest)

    return jax.shard_map(
        shards,
        mesh=mesh,
        in_specs=(
            P(("group", "tensor", "seq"), None),
            P(),
            P(("group", "tensor", "seq"), None),
            P(("group", "tensor", "seq"), None),
            P(("group", "tensor"), None, "seq"),
            P(("group", "tensor"), None, "seq"),
            P(("group", "tensor"), "seq", None),
            P("seq", None, None, ("group", "tensor"), None),
            P(),
        ),
        out_specs=(P(("group", "tensor", "seq"), None), P("seq", "tensor", "group", None)),
        check_vma=False,
    )
```

```python
import functools
import jax
import jax.numpy as jnp
from jax import lax
from jax.experimental import pallas as pl
from jax.experimental.pallas import tpu as pltpu
from jax.sharding import PartitionSpec as P

epsilon = 1e-06
LANES = 128
DENSE_TOKENS = 1024
WINDOW = 3
LINE = 8
RELAY_LAG = 3
SHARE_LAG = 4
LAST_LAG = 6
EASE = 16
UNIT = 32
DEEP = 32
PLANS = (
    (48, 48, 40, 40, 56, 48, 40, 32),
    (48, 48, 48, 48, 56, 56, 44, 32),
    (56, 48, 48, 40, 56, 56, 44, 32),
    (56, 56, 48, 48, 64, 56, 44, 32),
    (56, 56, 56, 56, 64, 60, 56, 44),
    (64, 64, 64, 64, 64, 64, 64, 64),
)
MESH = pl.DeviceIdType.MESH


def hand_over(prefill_key_value, lengths):
    layers_here, requests, heads, block, width = prefill_key_value.shape
    block_index = lax.axis_index("group") * lax.axis_size("tensor") + lax.axis_index("tensor")
    positions = block_index * block + jnp.arange(block, dtype=jnp.int32)
    keep = positions[None, :] < lengths[:, None]
    masked_entries = jnp.where(
        keep[None, :, None, :, None], prefill_key_value, jnp.zeros((), prefill_key_value.dtype)
    )
    flat = masked_entries.reshape(layers_here, requests * heads, block, width)
    return lax.all_to_all(flat, "tensor", split_axis=1, concat_axis=2, tiled=True)


def mixture(hidden_states, norm_gain, expert_ids, route_weights, w_gate, w_up, w_down):
    wide = hidden_states.astype(jnp.float32)
    scale = lax.rsqrt(jnp.mean(wide * wide, axis=1, keepdims=True) + epsilon)
    normed = (wide * scale * norm_gain.astype(jnp.float32)).astype(jnp.bfloat16)
    share = route_weights / jnp.sum(route_weights, axis=1, keepdims=True)
    expert_local, model_width, part_width = w_gate.shape
    sources = lax.axis_size("group") * lax.axis_size("tensor")
    experts = expert_local * sources
    rows_here, top_count = expert_ids.shape
    most = min(rows_here, max(2, 2 * rows_here * top_count // experts))
    flat_ids = expert_ids.reshape(-1)
    expert_grid = jnp.arange(experts, dtype=jnp.int32)
    onehot = (flat_ids[:, None] == expert_grid[None, :]).astype(jnp.int32)
    choices = jnp.arange(flat_ids.shape[0], dtype=jnp.int32)
    before = (choices[:, None] > choices[None, :]).astype(jnp.float32)
    earlier = jnp.dot(before, onehot.astype(jnp.float32), preferred_element_type=jnp.float32).astype(jnp.int32)
    position = jnp.sum(earlier * onehot, axis=1)
    target = flat_ids * most + position
    slot_grid = jnp.arange(experts * most, dtype=jnp.int32)
    hits = (target[:, None] == slot_grid[None, :]).reshape(rows_here, top_count, experts * most)
    select = jnp.sum(hits.astype(jnp.float32), axis=1).astype(jnp.bfloat16)
    mixing = jnp.sum(jnp.where(hits, share[:, :, None], 0.0), axis=1)
    outgoing = lax.dot_general(
        select, normed, (((0,), (0,)), ((), ())), preferred_element_type=jnp.float32
    )
    outgoing = outgoing.astype(jnp.bfloat16).reshape(experts, most, model_width)
    arrived = lax.all_to_all(outgoing, ("group", "tensor"), split_axis=0, concat_axis=0, tiled=True)
    arrived = arrived.reshape(sources, expert_local, most, model_width)
    pooled = lax.all_gather(arrived, "seq", axis=0, tiled=True)
    gate = jnp.einsum("semd,edf->semf", pooled, w_gate, preferred_element_type=jnp.float32)
    upper = jnp.einsum("semd,edf->semf", pooled, w_up, preferred_element_type=jnp.float32)
    active = (jax.nn.silu(gate) * upper).astype(jnp.bfloat16)
    summed = lax.psum_scatter(
        jnp.einsum("semf,efd->semd", active, w_down, preferred_element_type=jnp.float32).astype(
            jnp.bfloat16
        ),
        "seq",
        scatter_dimension=0,
        tiled=True,
    )
    returned = lax.all_to_all(
        summed.reshape(sources * expert_local, most, model_width),
        ("group", "tensor"),
        split_axis=0,
        concat_axis=0,
        tiled=True,
    )
    flat_back = returned.reshape(experts * most, model_width).astype(jnp.float32)
    mixed = jnp.dot(mixing, flat_back, precision=lax.Precision.HIGHEST)
    return mixed.astype(jnp.bfloat16)


def routed_shards(
    hidden_states, norm_gain, expert_ids, route_weights, w_gate, w_up, w_down, prefill_key_value, lengths
):
    moe_out = mixture(hidden_states, norm_gain, expert_ids, route_weights, w_gate, w_up, w_down)
    decoder_slot_cache = hand_over(prefill_key_value, lengths)
    return (moe_out, decoder_slot_cache)


def fused_kernel(
    sizes, caps, cuts,
    hidden_ref, gain_ref, ids_ref, weights_ref, gate_w, up_w, down_w, kv_ref, packed_ref,
    moe_ref, cache_ref, other_pool_ref,
    tokens, mixes, partial, gathered, folded, swapped, mate_out, mate_in, outgoing, returned,
    lend_first, lend_last,
    near_send, near_recv, far_send, far_recv, own_sem,
    stream_send, stream_recv, relay_send, share_send, share_recv, lend_send, lend_recv, lent_send, lent_recv,
    line_send, line_recv, pair_send, pair_recv, plane_send, plane_recv,
    part_send, part_recv, swap_send, swap_recv, mate_send, mate_recv, back_send, back_recv,
):
    groups, line, seqs = sizes
    plane = groups * seqs
    g, t, s = lax.axis_index("group"), lax.axis_index("tensor"), lax.axis_index("seq")
    here = g * seqs + s
    chips = line // 2
    chip, core = t // 2, lax.rem(t, 2)
    pair = (g, t + 1 - 2 * core, s)
    mate = chip + 1 - 2 * lax.rem(chip, 2)
    across, mate_across = lax.rem(chip + 2, chips), lax.rem(mate + 2, chips)
    mate_device, across_device = (g, mate * 2 + core, s), (g, across * 2 + core, s)
    layers, slots_all, block, _ = kv_ref.shape
    slots = slots_all // line
    rounds = layers * slots
    half_line = line // 2
    half, seat = t // half_line, lax.rem(t, half_line)
    far_half = 1 - half

    def in_line(step):
        other = lax.rem(t + step, line)
        return other, (g, other, s)

    def in_plane(step):
        other = lax.rem(here + step, plane)
        return other, (other // seqs, t, lax.rem(other, seqs))

    barrier = pltpu.get_barrier_semaphore()
    for step in range(1, line):
        pl.semaphore_signal(barrier, inc=1, device_id=in_line(step)[1], device_id_type=MESH)
    for step in range(1, plane):
        pl.semaphore_signal(barrier, inc=1, device_id=in_plane(step)[1], device_id_type=MESH)
    for k in range(half_line):
        pl.semaphore_signal(
            barrier, inc=1, device_id=(1 - g, far_half * half_line + k, s), device_id_type=MESH
        )

    columns = pl.ds(pl.multiple_of(t * block, block), block)
    own = pltpu.make_async_copy(
        kv_ref.at[:, pl.ds(t * slots, slots)], cache_ref.at[:, :, columns], own_sem
    )
    own.start()

    wide = hidden_ref[...].astype(jnp.float32)
    scale = lax.rsqrt(jnp.mean(wide * wide, axis=1, keepdims=True) + epsilon)
    tokens[here, chip, core] = (wide * scale * gain_ref[...].astype(jnp.float32)[None, :]).astype(jnp.bfloat16)
    top, rows = ids_ref.shape
    ids = ids_ref[...].T
    weights = weights_ref[...].T
    share = weights / jnp.sum(weights, axis=1, keepdims=True)
    lane = lax.broadcasted_iota(jnp.int32, (rows, LANES), 1)
    mix = jnp.zeros((rows, LANES), jnp.float32)
    for k in range(top):
        mix = mix + jnp.where(lane == ids[:, k : k + 1], share[:, k : k + 1], 0.0)
    mixes[here, chip, core] = mix

    pl.semaphore_wait(barrier, line + plane - 2 + half_line)

    def cap_of(device):
        total = 0
        for k in range(line):
            total = total + jnp.where(device == k, caps[k], 0)
        return total

    cap = cap_of(t)
    inner = jnp.logical_or(chip == 1, chip == 2)
    first_chip, last_chip = 1 + far_half * 1, far_half * 3
    lane_index = lax.rem(chip, 2)

    def pool(side, lane, entry):
        start = pl.multiple_of((side * DEEP + entry) * UNIT, UNIT)
        return cache_ref.at[:, pl.ds(lane * (slots // 2), slots // 2), pl.ds(start, UNIT)]

    def near_copy(index, step):
        other = half * half_line + lax.rem(seat + step, half_line)
        layer, slot = index // slots, lax.rem(index, slots)
        return pltpu.make_async_remote_copy(
            src_ref=kv_ref.at[layer, other * slots + slot],
            dst_ref=cache_ref.at[layer, slot, columns],
            send_sem=near_send.at[index, step],
            recv_sem=near_recv.at[index, step],
            device_id=(g, other, s),
            device_id_type=MESH,
        )

    def far_copy(layer, index, k, source):
        other = far_half * half_line + k
        at, slot = index // slots, lax.rem(index, slots)
        kept = block - cuts[layer]
        return pltpu.make_async_remote_copy(
            src_ref=kv_ref.at[at, other * slots + slot, pl.ds(0, kept)],
            dst_ref=cache_ref.at[at, slot, pl.ds(pl.multiple_of(t * block, block), kept)],
            send_sem=far_send.at[index, k],
            recv_sem=far_recv.at[index, source],
            device_id=(g, other, s),
            device_id_type=MESH,
        )

    def both_before(place, amount):
        return jnp.minimum(place, 2 * DEEP - amount)

    def entry_at(place, amount):
        rest = place - (2 * DEEP - amount)
        single = amount - DEEP
        swapped_turns = jnp.where(lax.rem(rest, 2) == 0, DEEP + rest // 2, rest // 2)
        head = single // 2
        turn = rest - head
        later = jnp.where(lax.rem(turn, 3) == 2, head + turn // 3, DEEP + turn - turn // 3)
        in_order = jnp.where(rest < head, rest, later)
        one = jnp.where(amount == 2 * DEEP, swapped_turns, in_order)
        return jnp.where(rest < 0, place + single, one)

    def stream_copy(place):
        entry = entry_at(place, cap)
        first = entry < DEEP
        target = jnp.where(first, entry, entry - (cap - DEEP))
        return pltpu.make_async_remote_copy(
            src_ref=packed_ref.at[entry],
            dst_ref=pool(half, lane_index, target),
            send_sem=stream_send.at[entry],
            recv_sem=stream_recv.at[lane_index, target],
            device_id=(g, jnp.where(first, first_chip, last_chip) * 2 + core, s),
            device_id_type=MESH,
        )

    def share_copy(lane, entry):
        return pltpu.make_async_remote_copy(
            src_ref=pool(far_half, lane, entry), dst_ref=other_pool_ref.at[lane, entry],
            send_sem=share_send.at[lane, entry], recv_sem=share_recv.at[lane, entry],
            device_id=pair, device_id_type=MESH,
        )

    def relay_copy(lane, entry, target):
        return pltpu.make_async_remote_copy(
            src_ref=pool(far_half, lane, entry), dst_ref=pool(far_half, lane, target),
            send_sem=relay_send.at[lane, entry], recv_sem=stream_recv.at[lane, target],
            device_id=mate_device, device_id_type=MESH,
        )

    def span_of(amount, index):
        at = jnp.clip(index, 0, rounds)
        after = jnp.clip(index + 1, 0, rounds)
        return amount * at // rounds, amount * after // rounds

    lends = [buffer for buffer in (lend_first, lend_last)]

    def lend_copy(layer):
        cut = cuts[layer]
        return pltpu.make_async_remote_copy(
            src_ref=kv_ref.at[layer, pl.ds(far_half * half_line * slots, half_line * slots), pl.ds(block - cut, cut)],
            dst_ref=lends[layer],
            send_sem=lend_send.at[layer], recv_sem=lend_recv.at[layer],
            device_id=(1 - g, t, s), device_id_type=MESH,
        )

    def lent_copy(layer, k, source):
        cut = cuts[layer]
        start = pl.multiple_of(t * block + block - cut, 16)
        return pltpu.make_async_remote_copy(
            src_ref=lends[layer].at[pl.ds(k * slots, slots)],
            dst_ref=cache_ref.at[layer, :, pl.ds(start, cut)],
            send_sem=lent_send.at[layer, k], recv_sem=lent_recv.at[layer, source],
            device_id=(1 - g, far_half * half_line + k, s), device_id_type=MESH,
        )

    lent_layers = [layer for layer in range(layers) if cuts[layer] > 0]

    def far_each(index, source, act):
        if cuts[0] == cuts[1]:
            for k in range(half_line):
                act(far_copy(0, index, k, k if source is None else source))
            return
        for layer in range(layers):
            @pl.when(index // slots == layer)
            def _():
                for k in range(half_line):
                    act(far_copy(layer, index, k, k if source is None else source))

    def near_span(index):
        return jnp.minimum(3 * index // 2, rounds), jnp.minimum(3 * (index + 1) // 2, rounds)

    def kv_start(index):
        @pl.loop(*near_span(index))
        def _(turn):
            for step in range(1, half_line):
                near_copy(turn, step).start()

        @pl.when(g == 0)
        def _():
            far_each(index, seat, lambda copy: copy.start())

        @pl.when(g == 1)
        def _():
            @pl.loop(*span_of(cap, index))
            def _(place):
                stream_copy(place).start()

    def kv_sent(index):
        @pl.loop(*near_span(index))
        def _(turn):
            for step in range(1, half_line):
                near_copy(turn, step).wait_send()

        @pl.when(g == 0)
        def _():
            far_each(index, seat, lambda copy: copy.wait_send())

        @pl.when(g == 1)
        def _():
            @pl.loop(*span_of(cap, index))
            def _(place):
                stream_copy(place).wait_send()

    def arrivals(index):
        @pl.when(g == 1)
        def _():
            for i in range(2):
                amount = cap_of(far_half * half_line + 2 * i + core)

                @pl.when(inner)
                def _():
                    low, high = span_of(amount, index - RELAY_LAG)

                    @pl.loop(both_before(low, amount), both_before(high, amount))
                    def _(place):
                        relay_copy(i, place + amount - DEEP, place + amount - DEEP).wait_recv()
                        relay_copy(i, place + amount - DEEP, place).start()

                @pl.loop(*span_of(amount, index - SHARE_LAG))
                def _(place):
                    entry = entry_at(place, amount)

                    @pl.when(jnp.logical_and(inner, entry < DEEP))
                    def _():
                        @pl.when(entry < amount - DEEP)
                        def _():
                            relay_copy(i, entry, entry).wait_recv()

                        share_copy(i, entry).start()

                    @pl.when(jnp.logical_and(jnp.logical_not(inner), entry >= DEEP))
                    def _():
                        at = entry - (amount - DEEP)
                        relay_copy(i, at, at).wait_recv()
                        share_copy(i, at).start()

                @pl.when(jnp.logical_not(inner))
                def _():
                    low, high = span_of(amount, index - LAST_LAG)

                    @pl.loop(both_before(low, amount), both_before(high, amount))
                    def _(place):
                        relay_copy(i, place, place).wait_recv()
                        share_copy(i, place).start()

    def line_copies(stage, place, device):
        return [
            pltpu.make_async_remote_copy(
                src_ref=ref.at[here, place, core], dst_ref=ref.at[here, place, core],
                send_sem=line_send.at[i, stage], recv_sem=line_recv.at[i, stage],
                device_id=device, device_id_type=MESH,
            )
            for i, ref in enumerate((tokens, mixes))
        ]

    over_copies = line_copies(0, chip, across_device)
    mate_copies = line_copies(1, chip, mate_device)
    relay_copies = line_copies(2, across, mate_device)

    pair_copies = [
        pltpu.make_async_remote_copy(
            src_ref=ref.at[here, :, core], dst_ref=ref.at[here, :, core],
            send_sem=pair_send.at[i], recv_sem=pair_recv.at[i],
            device_id=pair, device_id_type=MESH,
        )
        for i, ref in enumerate((tokens, mixes))
    ]

    swap = pltpu.make_async_remote_copy(
        src_ref=folded.at[:, 1 - core], dst_ref=swapped,
        send_sem=swap_send, recv_sem=swap_recv,
        device_id=pair, device_id_type=MESH,
    )

    def plane_copies(step):
        other, device = in_plane(step)
        return [
            pltpu.make_async_remote_copy(
                src_ref=ref.at[here], dst_ref=ref.at[here],
                send_sem=plane_send.at[i, step], recv_sem=plane_recv.at[i, step],
                device_id=device, device_id_type=MESH,
            )
            for i, ref in enumerate((tokens, mixes))
        ]

    def part_copy(step):
        other, device = in_plane(step)
        return pltpu.make_async_remote_copy(
            src_ref=partial.at[other], dst_ref=gathered.at[step],
            send_sem=part_send.at[step], recv_sem=part_recv.at[step],
            device_id=device, device_id_type=MESH,
        )

    mate_swap = pltpu.make_async_remote_copy(
        src_ref=mate_out, dst_ref=mate_in, send_sem=mate_send, recv_sem=mate_recv,
        device_id=mate_device, device_id_type=MESH,
    )
    back = pltpu.make_async_remote_copy(
        src_ref=outgoing, dst_ref=returned, send_sem=back_send, recv_sem=back_recv,
        device_id=across_device, device_id_type=MESH,
    )

    for copy in over_copies + mate_copies:
        copy.start()

    @pl.when(g == 0)
    def _():
        for layer in lent_layers:
            lend_copy(layer).start()

    spread = [c for step in range(1, plane) for c in plane_copies(step)]
    expert = g * line + t
    width = tokens.shape[-1]
    count = line * rows

    def across_done():
        for copy in over_copies:
            copy.wait()
        for copy in relay_copies:
            copy.start()

    def line_done():
        @pl.when(g == 1)
        def _():
            for layer in lent_layers:
                lend_copy(layer).wait_recv()
                for k in range(half_line):
                    lent_copy(layer, k, seat).start()

        for copy in mate_copies + relay_copies:
            copy.wait()
        for copy in pair_copies:
            copy.start()

    def pair_done():
        for copy in pair_copies:
            copy.wait()
        for copy in spread:
            copy.start()

    def spread_done():
        for copy in spread:
            copy.wait()

        @pl.loop(0, plane)
        def _(quarter):
            x = tokens[quarter].reshape(count, width)
            gate = jnp.dot(x, gate_w[0], preferred_element_type=jnp.float32)
            upper = jnp.dot(x, up_w[0], preferred_element_type=jnp.float32)
            active = (gate / (1.0 + jnp.exp(-gate)) * upper).astype(jnp.bfloat16)
            mixed = mixes[quarter].reshape(count, LANES)
            places = lax.broadcasted_iota(jnp.int32, (count, LANES), 1)
            weight = jnp.sum(jnp.where(places == expert, mixed, 0.0), axis=1, keepdims=True)
            out = jnp.dot(active, down_w[0], preferred_element_type=jnp.float32) * weight
            partial[quarter] = out.astype(jnp.bfloat16).reshape(chips, 2, rows, width)

        for step in range(1, plane):
            part_copy(step).start()

    def parts_done():
        for step in range(1, plane):
            part_copy(step).wait()

        @pl.loop(0, chips)
        def _(place):
            for side in range(2):
                total = partial[here, place, side].astype(jnp.float32)
                for step in range(1, plane):
                    total = total + gathered[step, place, side].astype(jnp.float32)
                folded[place, side] = total

        swap.start()

    def swap_done():
        swap.wait()
        mate_out[0] = folded[mate, core] + swapped[mate]
        mate_out[1] = folded[mate_across, core] + swapped[mate_across]
        mate_swap.start()

    def mate_done():
        mate_swap.wait()
        outgoing[...] = (folded[across, core] + swapped[across] + mate_in[1]).astype(jnp.bfloat16)
        back.start()

    def back_done():
        back.wait()
        total = folded[chip, core] + swapped[chip] + mate_in[0] + returned[...].astype(jnp.float32)
        moe_ref[...] = total.astype(jnp.bfloat16)

    stages = (across_done, line_done, pair_done, spread_done, parts_done, swap_done, mate_done, back_done)

    @pl.loop(0, rounds + LAST_LAG)
    def _(index):
        for i, stage in enumerate(stages):
            pl.when(index == WINDOW + (rounds - WINDOW) * (i + 1) // 9)(stage)

        @pl.when(jnp.logical_and(index >= WINDOW, index < rounds))
        def _():
            kv_sent(index - WINDOW)

        @pl.when(index < rounds)
        def _():
            kv_start(index)

        arrivals(index)

    @pl.loop(rounds - WINDOW, rounds)
    def _(index):
        kv_sent(index)

    @pl.when(g == 0)
    def _():
        @pl.loop(0, rounds)
        def _(index):
            far_each(index, None, lambda copy: copy.wait_recv())

        for layer in lent_layers:
            lend_copy(layer).wait_send()
            for k in range(half_line):
                lent_copy(layer, k, k).wait_recv()

    @pl.loop(0, rounds)
    def _(index):
        for step in range(1, half_line):
            near_copy(index, step).wait_recv()

    @pl.when(g == 1)
    def _():
        for layer in lent_layers:
            for k in range(half_line):
                lent_copy(layer, k, seat).wait_send()

        @pl.loop(0, DEEP)
        def _(entry):
            for i in range(2):
                share_copy(i, entry).wait()

        @pl.when(inner)
        def _():
            for i in range(2):
                amount = cap_of(far_half * half_line + 2 * i + core)

                @pl.loop(amount - DEEP, DEEP)
                def _(entry):
                    relay_copy(i, entry, entry).wait_send()

    own.wait()


def units_of(length, start, block):
    return jnp.clip((length - start + UNIT - 1) // UNIT, 0, block // UNIT)


def pack_kernel(heads, lengths_ref, kv_ref, packed_ref, chosen_ref, sems):
    layers, slots_all, block, width = kv_ref.shape
    requests = slots_all // heads
    quarter = requests // 4
    g, t = lax.axis_index("group"), lax.axis_index("tensor")
    start = (g * LINE + t) * block
    far_half = jnp.where(t < LINE // 2, 1, 0)

    def each(act, last, cap):
        chip = 1 + far_half if last == 0 else 3 * far_half

        def request(r, before):
            number = chip * quarter + r
            amount = units_of(lengths_ref[number], start, block)

            @pl.loop(0, amount)
            def _(q):
                k = before + q
                entry = k if last == 0 else cap - 1 - k
                act(number, q, entry)

            return before + amount

        lax.fori_loop(0, quarter, request, jnp.int32(0))

    def copy(number, q, entry):
        return pltpu.make_async_copy(
            kv_ref.at[:, pl.ds(number * heads, heads), pl.ds(pl.multiple_of(q * UNIT, UNIT), UNIT)],
            packed_ref.at[entry],
            sems.at[entry],
        )

    @pl.when(g == 1)
    def _():
        each(lambda *a: copy(*a).start(), 0, 0)

    misses = [jnp.int32(0) for _ in PLANS]
    for device in range(LINE):
        first = requests // 2 if device < LINE // 2 else 0
        needed = jnp.int32(0)
        for number in range(first, first + requests // 2):
            needed = needed + units_of(lengths_ref[number], (LINE + device) * block, block)
        for i, plan in enumerate(PLANS):
            misses[i] = misses[i] + jnp.where(needed > plan[device], 1, 0)
    chosen = jnp.int32(len(PLANS) - 1)
    for i in reversed(range(len(PLANS) - 1)):
        chosen = jnp.where(misses[i] == 0, i, chosen)
    chosen_ref[0] = chosen
    cap = jnp.int32(0)
    for i, plan in enumerate(PLANS):
        mine = jnp.int32(0)
        for device in range(LINE):
            mine = mine + jnp.where(t == device, plan[device], 0)
        cap = cap + jnp.where(chosen == i, mine, 0)

    @pl.when(g == 1)
    def _():
        each(lambda *a: copy(*a).start(), 1, cap)
        each(lambda *a: copy(*a).wait(), 0, 0)
        each(lambda *a: copy(*a).wait(), 1, cap)


def pack(lengths, kv, heads):
    layers, slots_all, block, width = kv.shape
    in_smem = pl.BlockSpec(memory_space=pltpu.SMEM)
    return pl.pallas_call(
        functools.partial(pack_kernel, heads),
        out_shape=(
            pltpu.VMEM((2 * DEEP, layers, heads, UNIT, width), kv.dtype),
            jax.ShapeDtypeStruct((1,), jnp.int32),
        ),
        in_specs=[in_smem, pl.BlockSpec(memory_space=pl.ANY)],
        out_specs=(pl.BlockSpec(memory_space=pltpu.VMEM), in_smem),
        scratch_shapes=[pltpu.SemaphoreType.DMA((2 * DEEP,))],
        compiler_params=pltpu.CompilerParams(vmem_limit_bytes=1024 * 1024),
    )(lengths, kv)


def mask_kernel(
    heads, piece,
    lengths_ref, cache_ref, other_pool_ref, moe_ref,
    out_ref, moe_out_ref,
    zeros, zero_unit, edges, edge_units, sems, unit_sems, moe_sem,
):
    layers, slots, span, width = cache_ref.shape
    pieces = span // piece
    half_line = pieces // 2
    per_device = slots // heads
    per_block = piece // UNIT
    g, t = lax.axis_index("group"), lax.axis_index("tensor")
    base = g * span
    half, core, chip = t // half_line, lax.rem(t, 2), t // 2
    inner = jnp.logical_or(chip == 1, chip == 2)
    moe_copy = pltpu.make_async_copy(moe_ref, moe_out_ref, moe_sem)
    moe_copy.start()
    zeros[...] = jnp.zeros(zeros.shape, zeros.dtype)
    zero_unit[...] = jnp.zeros(zero_unit.shape, zero_unit.dtype)
    places = lax.broadcasted_iota(jnp.int32, (piece, width), 0)
    unit_places = lax.broadcasted_iota(jnp.int32, zero_unit.shape, 2)
    direct_low = jnp.where(g == 0, 0, half * half_line)
    direct_high = jnp.where(g == 0, pieces, half * half_line + half_line)

    def rows_of(index):
        return pl.ds(pl.multiple_of(index * piece, piece), piece)

    def target(layer, r, index):
        return out_ref.at[layer, pl.ds(r * heads, heads), rows_of(index)]

    def unit_target(r, source, q):
        start = pl.multiple_of(source * piece + q * UNIT, UNIT)
        return out_ref.at[:, pl.ds(r * heads, heads), pl.ds(start, UNIT)]

    @pl.loop(0, per_device)
    def _(r):
        length = lengths_ref[per_device * t + r] - base
        group = pl.ds(r * heads, heads)

        @pl.loop(direct_low, direct_high)
        def _(index):
            left = length - index * piece

            @pl.when(left >= piece)
            def _():
                for layer in range(layers):
                    source = cache_ref.at[layer, group, rows_of(index)]
                    pltpu.make_async_copy(source, target(layer, r, index), sems.at[layer, r, index]).start()

            @pl.when(left <= 0)
            def _():
                for layer in range(layers):
                    pltpu.make_async_copy(zeros, target(layer, r, index), sems.at[layer, r, index]).start()

            @pl.when(jnp.logical_and(left > 0, left < piece))
            def _():
                for layer in range(layers):
                    @pl.loop(0, heads)
                    def _(head):
                        edges[layer, r * heads + head] = jnp.where(
                            places < left,
                            cache_ref[layer, r * heads + head, rows_of(index)],
                            jnp.zeros((), edges.dtype),
                        )

                    edge = edges.at[layer, group]
                    pltpu.make_async_copy(edge, target(layer, r, index), sems.at[layer, r, index]).start()

    @pl.when(g == 1)
    def _():
        @pl.loop(0, half_line)
        def _(k):
            source = (1 - half) * half_line + k
            start = base + source * piece
            before = jnp.int32(0)
            for r in range(2 * per_device):
                number = chip * 2 * per_device + r
                length = lengths_ref[number] - start
                mine = r - core * per_device

                @pl.when(jnp.logical_and(mine >= 0, mine < per_device))
                def _():
                    @pl.loop(0, per_block)
                    def _(q):
                        left = length - q * UNIT
                        order = before + q
                        entry = jnp.where(inner, order, DEEP - 1 - order)
                        rows = ((1 - half) * DEEP + entry) * UNIT
                        own_unit = cache_ref.at[
                            :, pl.ds((k // 2) * (slots // 2), slots // 2), pl.ds(pl.multiple_of(rows, UNIT), UNIT)
                        ]
                        at = unit_target(mine, source, q)
                        sem = unit_sems.at[mine, k, q]
                        for which, unit in enumerate((own_unit, other_pool_ref.at[k // 2, entry])):
                            here = (lax.rem(k, 2) == core) if which == 0 else (lax.rem(k, 2) != core)

                            @pl.when(jnp.logical_and(here, left >= UNIT))
                            def _():
                                pltpu.make_async_copy(unit, at, sem).start()

                            @pl.when(jnp.logical_and(here, jnp.logical_and(left > 0, left < UNIT)))
                            def _():
                                edge_units[mine] = jnp.where(
                                    unit_places < left, unit[...], jnp.zeros((), edges.dtype)
                                )
                                pltpu.make_async_copy(edge_units.at[mine], at, sem).start()

                        @pl.when(left <= 0)
                        def _():
                            pltpu.make_async_copy(zero_unit, at, sem).start()

                before = before + units_of(lengths_ref[number], start, piece)

    @pl.loop(0, per_device)
    def _(r):
        @pl.loop(direct_low, direct_high)
        def _(index):
            for layer in range(layers):
                pltpu.make_async_copy(zeros, target(layer, r, index), sems.at[layer, r, index]).wait()

    @pl.when(g == 1)
    def _():
        @pl.loop(0, half_line)
        def _(k):
            source = (1 - half) * half_line + k
            for mine in range(per_device):
                @pl.loop(0, per_block)
                def _(q):
                    at = unit_target(mine, source, q)
                    pltpu.make_async_copy(zero_unit, at, unit_sems.at[mine, k, q]).wait()

    moe_copy.wait()


def mask_cache(lengths, cache, other_pool, moe, heads, piece):
    layers, slots, span, width = cache.shape
    in_smem = pl.BlockSpec(memory_space=pltpu.SMEM)
    in_vmem = pl.BlockSpec(memory_space=pltpu.VMEM)
    cache, other_pool, moe = (
        pltpu.with_memory_space_constraint(x, pltpu.VMEM) for x in (cache, other_pool, moe)
    )
    in_place = pl.BlockSpec(memory_space=pl.ANY)
    unit = (layers, heads, UNIT, width)
    pieces = span // piece
    return pl.pallas_call(
        functools.partial(mask_kernel, heads, piece),
        out_shape=(
            jax.ShapeDtypeStruct(cache.shape, cache.dtype),
            jax.ShapeDtypeStruct(moe.shape, moe.dtype),
        ),
        in_specs=[in_smem, in_vmem, in_vmem, in_vmem],
        out_specs=(in_place, in_place),
        scratch_shapes=[
            pltpu.VMEM((heads, piece, width), cache.dtype),
            pltpu.VMEM(unit, cache.dtype),
            pltpu.VMEM((layers, slots, piece, width), cache.dtype),
            pltpu.VMEM((slots // heads, *unit), cache.dtype),
            pltpu.SemaphoreType.DMA((layers, slots // heads, pieces)),
            pltpu.SemaphoreType.DMA((slots // heads, pieces // 2, piece // UNIT)),
            pltpu.SemaphoreType.DMA,
        ],
        compiler_params=pltpu.CompilerParams(vmem_limit_bytes=4 * 1024 * 1024),
    )(lengths, cache, other_pool, moe)


def fused_shards(
    sizes,
    hidden_states, norm_gain, expert_ids, route_weights, w_gate, w_up, w_down, prefill_key_value, lengths,
):
    groups, line, seqs = sizes
    plane, chips = groups * seqs, line // 2
    layers, requests, heads, block, width = prefill_key_value.shape
    rows, model_width = hidden_states.shape
    slots = requests * heads // line
    rounds = layers * slots
    bf16 = jnp.bfloat16
    dma = pltpu.SemaphoreType.DMA
    in_vmem = pl.BlockSpec(memory_space=pltpu.VMEM)
    in_hbm = pl.BlockSpec(memory_space=pl.ANY)
    kv = prefill_key_value.reshape(layers, requests * heads, block, width)

    packed, chosen = pack(lengths, kv, heads)
    pool_type = pltpu.VMEM((2, DEEP, *packed.shape[1:]), bf16)

    def branch(number):
        caps = PLANS[number]
        spare = 2 * DEEP * 4 - max(sum(caps[: line // 2]), sum(caps[line // 2 :]))
        spare = spare - EASE if spare >= 4 * EASE else spare
        cuts = (spare // 32 * 16, (spare + 16) // 32 * 16)

        def run(hidden_states, norm_gain, ids, weights, w_gate, w_up, w_down, kv, packed, lengths):
            moe_out, cache, other_pool = pl.pallas_call(
                functools.partial(fused_kernel, sizes, caps, cuts),
                out_shape=(
                    pltpu.VMEM((rows, model_width), bf16),
                    pltpu.VMEM((layers, slots, line * block, width), bf16),
                    pool_type,
                ),
                in_specs=[in_vmem] * 7 + [in_hbm, in_vmem],
                out_specs=(in_vmem,) * 3,
                scratch_shapes=[
                    pltpu.VMEM((plane, chips, 2, rows, model_width), bf16),
                    pltpu.VMEM((plane, chips, 2, rows, LANES), jnp.float32),
                    pltpu.VMEM((plane, chips, 2, rows, model_width), bf16),
                    pltpu.VMEM((plane, chips, 2, rows, model_width), bf16),
                    pltpu.VMEM((chips, 2, rows, model_width), jnp.float32),
                    pltpu.VMEM((chips, rows, model_width), jnp.float32),
                    pltpu.VMEM((2, rows, model_width), jnp.float32),
                    pltpu.VMEM((2, rows, model_width), jnp.float32),
                    pltpu.VMEM((rows, model_width), bf16),
                    pltpu.VMEM((rows, model_width), bf16),
                    pltpu.VMEM((line // 2 * slots, max(16, cuts[0]), width), bf16),
                    pltpu.VMEM((line // 2 * slots, max(16, cuts[1]), width), bf16),
                    dma((rounds, line // 2)),
                    dma((rounds, line // 2)),
                    dma((rounds, line // 2)),
                    dma((rounds, line // 2)),
                    dma,
                    dma((2 * DEEP,)),
                    dma((2, DEEP)),
                    dma((2, DEEP)),
                    dma((2, DEEP)),
                    dma((2, DEEP)),
                    dma((2,)),
                    dma((2,)),
                    dma((2, line // 2)),
                    dma((2, line // 2)),
                    dma((2, 3)),
                    dma((2, 3)),
                    dma((2,)),
                    dma((2,)),
                    dma((2, plane)),
                    dma((2, plane)),
                    dma((plane,)),
                    dma((plane,)),
                    dma,
                    dma,
                    dma,
                    dma,
                    dma,
                    dma,
                ],
                compiler_params=pltpu.CompilerParams(
                    collective_id=number, has_side_effects=True, vmem_limit_bytes=15 * 1024 * 1024
                ),
            )(hidden_states, norm_gain, ids, weights, w_gate, w_up, w_down, kv, packed)
            return mask_cache(lengths, cache, other_pool, moe_out, heads, block)

        return run

    cache, moe_out = lax.switch(
        chosen[0],
        [branch(number) for number in range(len(PLANS))],
        hidden_states, norm_gain, expert_ids.T, route_weights.T, w_gate, w_up, w_down, kv, packed, lengths,
    )
    return (moe_out, cache)


def solution(mesh):
    sizes = tuple(mesh.shape[name] for name in ("group", "tensor", "seq"))

    def shards(hidden_states, *rest):
        tokens = hidden_states.shape[0] * sizes[0] * sizes[1] * sizes[2]
        one_expert = rest[3].shape[0] == 1 and sizes[0] * sizes[1] <= LANES
        layers, requests, heads, block, width = rest[6].shape
        regular = layers == 2 and requests == 2 * LINE and heads * requests == 8 * LINE and block == 8 * UNIT
        if tokens <= DENSE_TOKENS and one_expert and sizes == (2, LINE, 2) and regular:
            return fused_shards(sizes, hidden_states, *rest)
        return routed_shards(hidden_states, *rest)

    return jax.shard_map(
        shards,
        mesh=mesh,
        in_specs=(
            P(("group", "tensor", "seq"), None),
            P(),
            P(("group", "tensor", "seq"), None),
            P(("group", "tensor", "seq"), None),
            P(("group", "tensor"), None, "seq"),
            P(("group", "tensor"), None, "seq"),
            P(("group", "tensor"), "seq", None),
            P("seq", None, None, ("group", "tensor"), None),
            P(),
        ),
        out_specs=(P(("group", "tensor", "seq"), None), P("seq", "tensor", "group", None)),
        check_vma=False,
    )
```

```python
import functools
import jax
import jax.numpy as jnp
from jax import lax
from jax.experimental import pallas as pl
from jax.experimental.pallas import tpu as pltpu
from jax.sharding import PartitionSpec as P

epsilon = 1e-06
LANES = 128
DENSE_TOKENS = 1024
WINDOW = 3
LINE = 8
RELAY_LAG = 3
SHARE_LAG = 4
LAST_LAG = 6
EASE = 16
UNIT = 32
DEEP = 32
PLANS = (
    (48, 48, 40, 40, 56, 48, 40, 32),
    (48, 48, 48, 48, 56, 56, 44, 32),
    (56, 48, 48, 40, 56, 56, 44, 32),
    (56, 56, 48, 48, 64, 56, 44, 32),
    (56, 56, 56, 56, 64, 60, 56, 44),
    (64, 64, 64, 64, 64, 64, 64, 64),
)
MESH = pl.DeviceIdType.MESH


def hand_over(prefill_key_value, lengths):
    layers_here, requests, heads, block, width = prefill_key_value.shape
    block_index = lax.axis_index("group") * lax.axis_size("tensor") + lax.axis_index("tensor")
    positions = block_index * block + jnp.arange(block, dtype=jnp.int32)
    keep = positions[None, :] < lengths[:, None]
    masked_entries = jnp.where(
        keep[None, :, None, :, None], prefill_key_value, jnp.zeros((), prefill_key_value.dtype)
    )
    flat = masked_entries.reshape(layers_here, requests * heads, block, width)
    return lax.all_to_all(flat, "tensor", split_axis=1, concat_axis=2, tiled=True)


def mixture(hidden_states, norm_gain, expert_ids, route_weights, w_gate, w_up, w_down):
    wide = hidden_states.astype(jnp.float32)
    scale = lax.rsqrt(jnp.mean(wide * wide, axis=1, keepdims=True) + epsilon)
    normed = (wide * scale * norm_gain.astype(jnp.float32)).astype(jnp.bfloat16)
    share = route_weights / jnp.sum(route_weights, axis=1, keepdims=True)
    expert_local, model_width, part_width = w_gate.shape
    sources = lax.axis_size("group") * lax.axis_size("tensor")
    experts = expert_local * sources
    rows_here, top_count = expert_ids.shape
    most = min(rows_here, max(2, 2 * rows_here * top_count // experts))
    flat_ids = expert_ids.reshape(-1)
    expert_grid = jnp.arange(experts, dtype=jnp.int32)
    onehot = (flat_ids[:, None] == expert_grid[None, :]).astype(jnp.int32)
    choices = jnp.arange(flat_ids.shape[0], dtype=jnp.int32)
    before = (choices[:, None] > choices[None, :]).astype(jnp.float32)
    earlier = jnp.dot(before, onehot.astype(jnp.float32), preferred_element_type=jnp.float32).astype(jnp.int32)
    position = jnp.sum(earlier * onehot, axis=1)
    target = flat_ids * most + position
    slot_grid = jnp.arange(experts * most, dtype=jnp.int32)
    hits = (target[:, None] == slot_grid[None, :]).reshape(rows_here, top_count, experts * most)
    select = jnp.sum(hits.astype(jnp.float32), axis=1).astype(jnp.bfloat16)
    mixing = jnp.sum(jnp.where(hits, share[:, :, None], 0.0), axis=1)
    outgoing = lax.dot_general(
        select, normed, (((0,), (0,)), ((), ())), preferred_element_type=jnp.float32
    )
    outgoing = outgoing.astype(jnp.bfloat16).reshape(experts, most, model_width)
    arrived = lax.all_to_all(outgoing, ("group", "tensor"), split_axis=0, concat_axis=0, tiled=True)
    arrived = arrived.reshape(sources, expert_local, most, model_width)
    pooled = lax.all_gather(arrived, "seq", axis=0, tiled=True)
    gate = jnp.einsum("semd,edf->semf", pooled, w_gate, preferred_element_type=jnp.float32)
    upper = jnp.einsum("semd,edf->semf", pooled, w_up, preferred_element_type=jnp.float32)
    active = (jax.nn.silu(gate) * upper).astype(jnp.bfloat16)
    summed = lax.psum_scatter(
        jnp.einsum("semf,efd->semd", active, w_down, preferred_element_type=jnp.float32).astype(
            jnp.bfloat16
        ),
        "seq",
        scatter_dimension=0,
        tiled=True,
    )
    returned = lax.all_to_all(
        summed.reshape(sources * expert_local, most, model_width),
        ("group", "tensor"),
        split_axis=0,
        concat_axis=0,
        tiled=True,
    )
    flat_back = returned.reshape(experts * most, model_width).astype(jnp.float32)
    mixed = jnp.dot(mixing, flat_back, precision=lax.Precision.HIGHEST)
    return mixed.astype(jnp.bfloat16)


def routed_shards(
    hidden_states, norm_gain, expert_ids, route_weights, w_gate, w_up, w_down, prefill_key_value, lengths
):
    moe_out = mixture(hidden_states, norm_gain, expert_ids, route_weights, w_gate, w_up, w_down)
    decoder_slot_cache = hand_over(prefill_key_value, lengths)
    return (moe_out, decoder_slot_cache)


def fused_kernel(
    sizes, caps, cuts,
    hidden_ref, gain_ref, ids_ref, weights_ref, gate_w, up_w, down_w, kv_ref, packed_ref,
    moe_ref, cache_ref, other_pool_ref,
    tokens, mixes, partial, gathered, folded, swapped, mate_out, mate_in, outgoing, returned,
    lend_first, lend_last,
    near_send, near_recv, far_send, far_recv, own_sem,
    stream_send, stream_recv, relay_send, share_send, share_recv, lend_send, lend_recv, lent_send, lent_recv,
    line_send, line_recv, pair_send, pair_recv, plane_send, plane_recv,
    part_send, part_recv, swap_send, swap_recv, mate_send, mate_recv, back_send, back_recv,
):
    groups, line, seqs = sizes
    plane = groups * seqs
    g, t, s = lax.axis_index("group"), lax.axis_index("tensor"), lax.axis_index("seq")
    here = g * seqs + s
    chips = line // 2
    chip, core = t // 2, lax.rem(t, 2)
    pair = (g, t + 1 - 2 * core, s)
    mate = chip + 1 - 2 * lax.rem(chip, 2)
    across, mate_across = lax.rem(chip + 2, chips), lax.rem(mate + 2, chips)
    mate_device, across_device = (g, mate * 2 + core, s), (g, across * 2 + core, s)
    layers, slots_all, block, _ = kv_ref.shape
    slots = slots_all // line
    rounds = layers * slots
    half_line = line // 2
    half, seat = t // half_line, lax.rem(t, half_line)
    far_half = 1 - half

    def in_line(step):
        other = lax.rem(t + step, line)
        return other, (g, other, s)

    def in_plane(step):
        other = lax.rem(here + step, plane)
        return other, (other // seqs, t, lax.rem(other, seqs))

    barrier = pltpu.get_barrier_semaphore()
    for step in range(1, line):
        pl.semaphore_signal(barrier, inc=1, device_id=in_line(step)[1], device_id_type=MESH)
    for step in range(1, plane):
        pl.semaphore_signal(barrier, inc=1, device_id=in_plane(step)[1], device_id_type=MESH)
    for k in range(half_line):
        pl.semaphore_signal(
            barrier, inc=1, device_id=(1 - g, far_half * half_line + k, s), device_id_type=MESH
        )

    columns = pl.ds(pl.multiple_of(t * block, block), block)
    own = pltpu.make_async_copy(
        kv_ref.at[:, pl.ds(t * slots, slots)], cache_ref.at[:, :, columns], own_sem
    )
    own.start()

    wide = hidden_ref[...].astype(jnp.float32)
    scale = lax.rsqrt(jnp.mean(wide * wide, axis=1, keepdims=True) + epsilon)
    tokens[here, chip, core] = (wide * scale * gain_ref[...].astype(jnp.float32)[None, :]).astype(jnp.bfloat16)
    top, rows = ids_ref.shape
    ids = ids_ref[...].T
    weights = weights_ref[...].T
    share = weights / jnp.sum(weights, axis=1, keepdims=True)
    lane = lax.broadcasted_iota(jnp.int32, (rows, LANES), 1)
    mix = jnp.zeros((rows, LANES), jnp.float32)
    for k in range(top):
        mix = mix + jnp.where(lane == ids[:, k : k + 1], share[:, k : k + 1], 0.0)
    mixes[here, chip, core] = mix

    pl.semaphore_wait(barrier, line + plane - 2 + half_line)

    def cap_of(device):
        total = 0
        for k in range(line):
            total = total + jnp.where(device == k, caps[k], 0)
        return total

    cap = cap_of(t)
    inner = jnp.logical_or(chip == 1, chip == 2)
    first_chip, last_chip = 1 + far_half * 1, far_half * 3
    lane_index = lax.rem(chip, 2)

    def pool(side, lane, entry):
        start = pl.multiple_of((side * DEEP + entry) * UNIT, UNIT)
        return cache_ref.at[:, pl.ds(lane * (slots // 2), slots // 2), pl.ds(start, UNIT)]

    def near_copy(index, step):
        other = half * half_line + lax.rem(seat + step, half_line)
        layer, slot = index // slots, lax.rem(index, slots)
        return pltpu.make_async_remote_copy(
            src_ref=kv_ref.at[layer, other * slots + slot],
            dst_ref=cache_ref.at[layer, slot, columns],
            send_sem=near_send.at[index, step],
            recv_sem=near_recv.at[index, step],
            device_id=(g, other, s),
            device_id_type=MESH,
        )

    def far_copy(layer, index, k, source):
        other = far_half * half_line + k
        at, slot = index // slots, lax.rem(index, slots)
        kept = block - cuts[layer]
        return pltpu.make_async_remote_copy(
            src_ref=kv_ref.at[at, other * slots + slot, pl.ds(0, kept)],
            dst_ref=cache_ref.at[at, slot, pl.ds(pl.multiple_of(t * block, block), kept)],
            send_sem=far_send.at[index, k],
            recv_sem=far_recv.at[index, source],
            device_id=(g, other, s),
            device_id_type=MESH,
        )

    def both_before(place, amount):
        return jnp.minimum(place, 2 * DEEP - amount)

    def entry_at(place, amount):
        rest = place - (2 * DEEP - amount)
        single = amount - DEEP
        swapped_turns = jnp.where(lax.rem(rest, 2) == 0, DEEP + rest // 2, rest // 2)
        head = single // 2
        turn = rest - head
        later = jnp.where(lax.rem(turn, 3) == 2, head + turn // 3, DEEP + turn - turn // 3)
        in_order = jnp.where(rest < head, rest, later)
        one = jnp.where(amount == 2 * DEEP, swapped_turns, in_order)
        return jnp.where(rest < 0, place + single, one)

    def stream_copy(place):
        entry = entry_at(place, cap)
        first = entry < DEEP
        target = jnp.where(first, entry, entry - (cap - DEEP))
        return pltpu.make_async_remote_copy(
            src_ref=packed_ref.at[entry],
            dst_ref=pool(half, lane_index, target),
            send_sem=stream_send.at[entry],
            recv_sem=stream_recv.at[lane_index, target],
            device_id=(g, jnp.where(first, first_chip, last_chip) * 2 + core, s),
            device_id_type=MESH,
        )

    def share_copy(lane, entry):
        return pltpu.make_async_remote_copy(
            src_ref=pool(far_half, lane, entry), dst_ref=other_pool_ref.at[lane, entry],
            send_sem=share_send.at[lane, entry], recv_sem=share_recv.at[lane, entry],
            device_id=pair, device_id_type=MESH,
        )

    def relay_copy(lane, entry, target):
        return pltpu.make_async_remote_copy(
            src_ref=pool(far_half, lane, entry), dst_ref=pool(far_half, lane, target),
            send_sem=relay_send.at[lane, entry], recv_sem=stream_recv.at[lane, target],
            device_id=mate_device, device_id_type=MESH,
        )

    def span_of(amount, index):
        at = jnp.clip(index, 0, rounds)
        after = jnp.clip(index + 1, 0, rounds)
        return amount * at // rounds, amount * after // rounds

    lends = [buffer for buffer in (lend_first, lend_last)]

    def lend_copy(layer):
        cut = cuts[layer]
        return pltpu.make_async_remote_copy(
            src_ref=kv_ref.at[layer, pl.ds(far_half * half_line * slots, half_line * slots), pl.ds(block - cut, cut)],
            dst_ref=lends[layer],
            send_sem=lend_send.at[layer], recv_sem=lend_recv.at[layer],
            device_id=(1 - g, t, s), device_id_type=MESH,
        )

    def lent_copy(layer, k, source):
        cut = cuts[layer]
        start = pl.multiple_of(t * block + block - cut, 16)
        return pltpu.make_async_remote_copy(
            src_ref=lends[layer].at[pl.ds(k * slots, slots)],
            dst_ref=cache_ref.at[layer, :, pl.ds(start, cut)],
            send_sem=lent_send.at[layer, k], recv_sem=lent_recv.at[layer, source],
            device_id=(1 - g, far_half * half_line + k, s), device_id_type=MESH,
        )

    lent_layers = [layer for layer in range(layers) if cuts[layer] > 0]

    def far_each(index, source, act):
        if cuts[0] == cuts[1]:
            for k in range(half_line):
                act(far_copy(0, index, k, k if source is None else source))
            return
        for layer in range(layers):
            @pl.when(index // slots == layer)
            def _():
                for k in range(half_line):
                    act(far_copy(layer, index, k, k if source is None else source))

    def near_span(index):
        return jnp.minimum(3 * index // 2, rounds), jnp.minimum(3 * (index + 1) // 2, rounds)

    def kv_start(index):
        @pl.loop(*near_span(index))
        def _(turn):
            for step in range(1, half_line):
                near_copy(turn, step).start()

        @pl.when(g == 0)
        def _():
            far_each(index, seat, lambda copy: copy.start())

        @pl.when(g == 1)
        def _():
            @pl.loop(*span_of(cap, index))
            def _(place):
                stream_copy(place).start()

    def kv_sent(index):
        @pl.loop(*near_span(index))
        def _(turn):
            for step in range(1, half_line):
                near_copy(turn, step).wait_send()

        @pl.when(g == 0)
        def _():
            far_each(index, seat, lambda copy: copy.wait_send())

        @pl.when(g == 1)
        def _():
            @pl.loop(*span_of(cap, index))
            def _(place):
                stream_copy(place).wait_send()

    def arrivals(index):
        @pl.when(g == 1)
        def _():
            for i in range(2):
                amount = cap_of(far_half * half_line + 2 * i + core)

                @pl.when(inner)
                def _():
                    low, high = span_of(amount, index - RELAY_LAG)

                    @pl.loop(both_before(low, amount), both_before(high, amount))
                    def _(place):
                        relay_copy(i, place + amount - DEEP, place + amount - DEEP).wait_recv()
                        relay_copy(i, place + amount - DEEP, place).start()

                @pl.loop(*span_of(amount, index - SHARE_LAG))
                def _(place):
                    entry = entry_at(place, amount)

                    @pl.when(jnp.logical_and(inner, entry < DEEP))
                    def _():
                        @pl.when(entry < amount - DEEP)
                        def _():
                            relay_copy(i, entry, entry).wait_recv()

                        share_copy(i, entry).start()

                    @pl.when(jnp.logical_and(jnp.logical_not(inner), entry >= DEEP))
                    def _():
                        at = entry - (amount - DEEP)
                        relay_copy(i, at, at).wait_recv()
                        share_copy(i, at).start()

                @pl.when(jnp.logical_not(inner))
                def _():
                    low, high = span_of(amount, index - LAST_LAG)

                    @pl.loop(both_before(low, amount), both_before(high, amount))
                    def _(place):
                        relay_copy(i, place, place).wait_recv()
                        share_copy(i, place).start()

    def line_copies(stage, place, device):
        return [
            pltpu.make_async_remote_copy(
                src_ref=ref.at[here, place, core], dst_ref=ref.at[here, place, core],
                send_sem=line_send.at[i, stage], recv_sem=line_recv.at[i, stage],
                device_id=device, device_id_type=MESH,
            )
            for i, ref in enumerate((tokens, mixes))
        ]

    over_copies = line_copies(0, chip, across_device)
    mate_copies = line_copies(1, chip, mate_device)
    relay_copies = line_copies(2, across, mate_device)

    pair_copies = [
        pltpu.make_async_remote_copy(
            src_ref=ref.at[here, :, core], dst_ref=ref.at[here, :, core],
            send_sem=pair_send.at[i], recv_sem=pair_recv.at[i],
            device_id=pair, device_id_type=MESH,
        )
        for i, ref in enumerate((tokens, mixes))
    ]

    swap = pltpu.make_async_remote_copy(
        src_ref=folded.at[:, 1 - core], dst_ref=swapped,
        send_sem=swap_send, recv_sem=swap_recv,
        device_id=pair, device_id_type=MESH,
    )

    def plane_copies(step):
        other, device = in_plane(step)
        return [
            pltpu.make_async_remote_copy(
                src_ref=ref.at[here], dst_ref=ref.at[here],
                send_sem=plane_send.at[i, step], recv_sem=plane_recv.at[i, step],
                device_id=device, device_id_type=MESH,
            )
            for i, ref in enumerate((tokens, mixes))
        ]

    def part_copy(step):
        other, device = in_plane(step)
        return pltpu.make_async_remote_copy(
            src_ref=partial.at[other], dst_ref=gathered.at[step],
            send_sem=part_send.at[step], recv_sem=part_recv.at[step],
            device_id=device, device_id_type=MESH,
        )

    mate_swap = pltpu.make_async_remote_copy(
        src_ref=mate_out, dst_ref=mate_in, send_sem=mate_send, recv_sem=mate_recv,
        device_id=mate_device, device_id_type=MESH,
    )
    back = pltpu.make_async_remote_copy(
        src_ref=outgoing, dst_ref=returned, send_sem=back_send, recv_sem=back_recv,
        device_id=across_device, device_id_type=MESH,
    )

    for copy in over_copies + mate_copies:
        copy.start()

    @pl.when(g == 0)
    def _():
        for layer in lent_layers:
            lend_copy(layer).start()

    spread = [c for step in range(1, plane) for c in plane_copies(step)]
    expert = g * line + t
    width = tokens.shape[-1]
    count = line * rows

    def across_done():
        for copy in over_copies:
            copy.wait()
        for copy in relay_copies:
            copy.start()

    def line_done():
        @pl.when(g == 1)
        def _():
            for layer in lent_layers:
                lend_copy(layer).wait_recv()
                for k in range(half_line):
                    lent_copy(layer, k, seat).start()

        for copy in mate_copies + relay_copies:
            copy.wait()
        for copy in pair_copies:
            copy.start()

    def pair_done():
        for copy in pair_copies:
            copy.wait()
        for copy in spread:
            copy.start()

    def spread_done():
        for copy in spread:
            copy.wait()

        @pl.loop(0, plane)
        def _(quarter):
            x = tokens[quarter].reshape(count, width)
            gate = jnp.dot(x, gate_w[0], preferred_element_type=jnp.float32)
            upper = jnp.dot(x, up_w[0], preferred_element_type=jnp.float32)
            active = (gate / (1.0 + jnp.exp(-gate)) * upper).astype(jnp.bfloat16)
            mixed = mixes[quarter].reshape(count, LANES)
            places = lax.broadcasted_iota(jnp.int32, (count, LANES), 1)
            weight = jnp.sum(jnp.where(places == expert, mixed, 0.0), axis=1, keepdims=True)
            out = jnp.dot(active, down_w[0], preferred_element_type=jnp.float32) * weight
            partial[quarter] = out.astype(jnp.bfloat16).reshape(chips, 2, rows, width)

        for step in range(1, plane):
            part_copy(step).start()

    def parts_done():
        for step in range(1, plane):
            part_copy(step).wait()

        @pl.loop(0, chips)
        def _(place):
            for side in range(2):
                total = partial[here, place, side].astype(jnp.float32)
                for step in range(1, plane):
                    total = total + gathered[step, place, side].astype(jnp.float32)
                folded[place, side] = total

        swap.start()

    def swap_done():
        swap.wait()
        mate_out[0] = folded[mate, core] + swapped[mate]
        mate_out[1] = folded[mate_across, core] + swapped[mate_across]
        mate_swap.start()

    def mate_done():
        mate_swap.wait()
        outgoing[...] = (folded[across, core] + swapped[across] + mate_in[1]).astype(jnp.bfloat16)
        back.start()

    def back_done():
        back.wait()
        total = folded[chip, core] + swapped[chip] + mate_in[0] + returned[...].astype(jnp.float32)
        moe_ref[...] = total.astype(jnp.bfloat16)

    stages = (across_done, line_done, pair_done, spread_done, parts_done, swap_done, mate_done, back_done)

    @pl.loop(0, rounds + LAST_LAG)
    def _(index):
        for i, stage in enumerate(stages):
            pl.when(index == WINDOW + (rounds - WINDOW) * (i + 1) // 9)(stage)

        @pl.when(jnp.logical_and(index >= WINDOW, index < rounds))
        def _():
            kv_sent(index - WINDOW)

        @pl.when(index < rounds)
        def _():
            kv_start(index)

        arrivals(index)

    @pl.loop(rounds - WINDOW, rounds)
    def _(index):
        kv_sent(index)

    @pl.when(g == 0)
    def _():
        @pl.loop(0, rounds)
        def _(index):
            far_each(index, None, lambda copy: copy.wait_recv())

        for layer in lent_layers:
            lend_copy(layer).wait_send()
            for k in range(half_line):
                lent_copy(layer, k, k).wait_recv()

    @pl.loop(0, rounds)
    def _(index):
        for step in range(1, half_line):
            near_copy(index, step).wait_recv()

    @pl.when(g == 1)
    def _():
        for layer in lent_layers:
            for k in range(half_line):
                lent_copy(layer, k, seat).wait_send()

        @pl.loop(0, DEEP)
        def _(entry):
            for i in range(2):
                share_copy(i, entry).wait()

        @pl.when(inner)
        def _():
            for i in range(2):
                amount = cap_of(far_half * half_line + 2 * i + core)

                @pl.loop(amount - DEEP, DEEP)
                def _(entry):
                    relay_copy(i, entry, entry).wait_send()

    own.wait()


def units_of(length, start, block):
    return jnp.clip((length - start + UNIT - 1) // UNIT, 0, block // UNIT)


def pack_kernel(heads, lengths_ref, kv_ref, packed_ref, chosen_ref, sems):
    layers, slots_all, block, width = kv_ref.shape
    requests = slots_all // heads
    quarter = requests // 4
    g, t = lax.axis_index("group"), lax.axis_index("tensor")
    start = (g * LINE + t) * block
    far_half = jnp.where(t < LINE // 2, 1, 0)

    def each(act, last, cap):
        chip = 1 + far_half if last == 0 else 3 * far_half

        def request(r, before):
            number = chip * quarter + r
            amount = units_of(lengths_ref[number], start, block)

            @pl.loop(0, amount)
            def _(q):
                k = before + q
                entry = k if last == 0 else cap - 1 - k
                act(number, q, entry)

            return before + amount

        lax.fori_loop(0, quarter, request, jnp.int32(0))

    def copy(number, q, entry):
        return pltpu.make_async_copy(
            kv_ref.at[:, pl.ds(number * heads, heads), pl.ds(pl.multiple_of(q * UNIT, UNIT), UNIT)],
            packed_ref.at[entry],
            sems.at[entry],
        )

    @pl.when(g == 1)
    def _():
        each(lambda *a: copy(*a).start(), 0, 0)

    misses = [jnp.int32(0) for _ in PLANS]
    for device in range(LINE):
        first = requests // 2 if device < LINE // 2 else 0
        needed = jnp.int32(0)
        for number in range(first, first + requests // 2):
            needed = needed + units_of(lengths_ref[number], (LINE + device) * block, block)
        for i, plan in enumerate(PLANS):
            misses[i] = misses[i] + jnp.where(needed > plan[device], 1, 0)
    chosen = jnp.int32(len(PLANS) - 1)
    for i in reversed(range(len(PLANS) - 1)):
        chosen = jnp.where(misses[i] == 0, i, chosen)
    chosen_ref[0] = chosen
    cap = jnp.int32(0)
    for i, plan in enumerate(PLANS):
        mine = jnp.int32(0)
        for device in range(LINE):
            mine = mine + jnp.where(t == device, plan[device], 0)
        cap = cap + jnp.where(chosen == i, mine, 0)

    @pl.when(g == 1)
    def _():
        each(lambda *a: copy(*a).start(), 1, cap)
        each(lambda *a: copy(*a).wait(), 0, 0)
        each(lambda *a: copy(*a).wait(), 1, cap)


def pack(lengths, kv, heads):
    layers, slots_all, block, width = kv.shape
    in_smem = pl.BlockSpec(memory_space=pltpu.SMEM)
    return pl.pallas_call(
        functools.partial(pack_kernel, heads),
        out_shape=(
            pltpu.VMEM((2 * DEEP, layers, heads, UNIT, width), kv.dtype),
            jax.ShapeDtypeStruct((1,), jnp.int32),
        ),
        in_specs=[in_smem, pl.BlockSpec(memory_space=pl.ANY)],
        out_specs=(pl.BlockSpec(memory_space=pltpu.VMEM), in_smem),
        scratch_shapes=[pltpu.SemaphoreType.DMA((2 * DEEP,))],
        compiler_params=pltpu.CompilerParams(vmem_limit_bytes=1024 * 1024),
    )(lengths, kv)


def mask_kernel(
    heads, piece,
    lengths_ref, cache_ref, other_pool_ref, moe_ref,
    out_ref, moe_out_ref,
    zeros, zero_unit, edges, edge_units, sems, unit_sems, moe_sem,
):
    layers, slots, span, width = cache_ref.shape
    pieces = span // piece
    half_line = pieces // 2
    per_device = slots // heads
    per_block = piece // UNIT
    g, t = lax.axis_index("group"), lax.axis_index("tensor")
    base = g * span
    half, core, chip = t // half_line, lax.rem(t, 2), t // 2
    inner = jnp.logical_or(chip == 1, chip == 2)
    moe_copy = pltpu.make_async_copy(moe_ref, moe_out_ref, moe_sem)
    moe_copy.start()
    zeros[...] = jnp.zeros(zeros.shape, zeros.dtype)
    zero_unit[...] = jnp.zeros(zero_unit.shape, zero_unit.dtype)
    places = lax.broadcasted_iota(jnp.int32, (piece, width), 0)
    unit_places = lax.broadcasted_iota(jnp.int32, zero_unit.shape, 2)
    direct_low = jnp.where(g == 0, 0, half * half_line)
    direct_high = jnp.where(g == 0, pieces, half * half_line + half_line)

    def rows_of(index):
        return pl.ds(pl.multiple_of(index * piece, piece), piece)

    def target(layer, r, index):
        return out_ref.at[layer, pl.ds(r * heads, heads), rows_of(index)]

    def unit_target(r, source, q):
        start = pl.multiple_of(source * piece + q * UNIT, UNIT)
        return out_ref.at[:, pl.ds(r * heads, heads), pl.ds(start, UNIT)]

    @pl.loop(0, per_device)
    def _(r):
        length = lengths_ref[per_device * t + r] - base
        group = pl.ds(r * heads, heads)

        @pl.loop(direct_low, direct_high)
        def _(index):
            left = length - index * piece

            @pl.when(left >= piece)
            def _():
                for layer in range(layers):
                    source = cache_ref.at[layer, group, rows_of(index)]
                    pltpu.make_async_copy(source, target(layer, r, index), sems.at[layer, r, index]).start()

            @pl.when(left <= 0)
            def _():
                for layer in range(layers):
                    pltpu.make_async_copy(zeros, target(layer, r, index), sems.at[layer, r, index]).start()

            @pl.when(jnp.logical_and(left > 0, left < piece))
            def _():
                for layer in range(layers):
                    @pl.loop(0, heads)
                    def _(head):
                        edges[layer, r * heads + head] = jnp.where(
                            places < left,
                            cache_ref[layer, r * heads + head, rows_of(index)],
                            jnp.zeros((), edges.dtype),
                        )

                    edge = edges.at[layer, group]
                    pltpu.make_async_copy(edge, target(layer, r, index), sems.at[layer, r, index]).start()

    @pl.when(g == 1)
    def _():
        @pl.loop(0, half_line)
        def _(k):
            source = (1 - half) * half_line + k
            start = base + source * piece
            before = jnp.int32(0)
            for r in range(2 * per_device):
                number = chip * 2 * per_device + r
                length = lengths_ref[number] - start
                mine = r - core * per_device

                @pl.when(jnp.logical_and(mine >= 0, mine < per_device))
                def _():
                    @pl.loop(0, per_block)
                    def _(q):
                        left = length - q * UNIT
                        order = before + q
                        entry = jnp.where(inner, order, DEEP - 1 - order)
                        rows = ((1 - half) * DEEP + entry) * UNIT
                        own_unit = cache_ref.at[
                            :, pl.ds((k // 2) * (slots // 2), slots // 2), pl.ds(pl.multiple_of(rows, UNIT), UNIT)
                        ]
                        at = unit_target(mine, source, q)
                        sem = unit_sems.at[mine, k, q]
                        for which, unit in enumerate((own_unit, other_pool_ref.at[k // 2, entry])):
                            here = (lax.rem(k, 2) == core) if which == 0 else (lax.rem(k, 2) != core)

                            @pl.when(jnp.logical_and(here, left >= UNIT))
                            def _():
                                pltpu.make_async_copy(unit, at, sem).start()

                            @pl.when(jnp.logical_and(here, jnp.logical_and(left > 0, left < UNIT)))
                            def _():
                                edge_units[mine] = jnp.where(
                                    unit_places < left, unit[...], jnp.zeros((), edges.dtype)
                                )
                                pltpu.make_async_copy(edge_units.at[mine], at, sem).start()

                        @pl.when(left <= 0)
                        def _():
                            pltpu.make_async_copy(zero_unit, at, sem).start()

                before = before + units_of(lengths_ref[number], start, piece)

    @pl.loop(0, per_device)
    def _(r):
        @pl.loop(direct_low, direct_high)
        def _(index):
            for layer in range(layers):
                pltpu.make_async_copy(zeros, target(layer, r, index), sems.at[layer, r, index]).wait()

    @pl.when(g == 1)
    def _():
        @pl.loop(0, half_line)
        def _(k):
            source = (1 - half) * half_line + k
            for mine in range(per_device):
                @pl.loop(0, per_block)
                def _(q):
                    at = unit_target(mine, source, q)
                    pltpu.make_async_copy(zero_unit, at, unit_sems.at[mine, k, q]).wait()

    moe_copy.wait()


def mask_cache(lengths, cache, other_pool, moe, heads, piece):
    layers, slots, span, width = cache.shape
    in_smem = pl.BlockSpec(memory_space=pltpu.SMEM)
    in_vmem = pl.BlockSpec(memory_space=pltpu.VMEM)
    cache, other_pool, moe = (
        pltpu.with_memory_space_constraint(x, pltpu.VMEM) for x in (cache, other_pool, moe)
    )
    in_place = pl.BlockSpec(memory_space=pl.ANY)
    unit = (layers, heads, UNIT, width)
    pieces = span // piece
    return pl.pallas_call(
        functools.partial(mask_kernel, heads, piece),
        out_shape=(
            jax.ShapeDtypeStruct(cache.shape, cache.dtype),
            jax.ShapeDtypeStruct(moe.shape, moe.dtype),
        ),
        in_specs=[in_smem, in_vmem, in_vmem, in_vmem],
        out_specs=(in_place, in_place),
        scratch_shapes=[
            pltpu.VMEM((heads, piece, width), cache.dtype),
            pltpu.VMEM(unit, cache.dtype),
            pltpu.VMEM((layers, slots, piece, width), cache.dtype),
            pltpu.VMEM((slots // heads, *unit), cache.dtype),
            pltpu.SemaphoreType.DMA((layers, slots // heads, pieces)),
            pltpu.SemaphoreType.DMA((slots // heads, pieces // 2, piece // UNIT)),
            pltpu.SemaphoreType.DMA,
        ],
        compiler_params=pltpu.CompilerParams(vmem_limit_bytes=4 * 1024 * 1024),
    )(lengths, cache, other_pool, moe)


def fused_shards(
    sizes,
    hidden_states, norm_gain, expert_ids, route_weights, w_gate, w_up, w_down, prefill_key_value, lengths,
):
    groups, line, seqs = sizes
    plane, chips = groups * seqs, line // 2
    layers, requests, heads, block, width = prefill_key_value.shape
    rows, model_width = hidden_states.shape
    slots = requests * heads // line
    rounds = layers * slots
    bf16 = jnp.bfloat16
    dma = pltpu.SemaphoreType.DMA
    in_vmem = pl.BlockSpec(memory_space=pltpu.VMEM)
    in_hbm = pl.BlockSpec(memory_space=pl.ANY)
    kv = prefill_key_value.reshape(layers, requests * heads, block, width)

    packed, chosen = pack(lengths, kv, heads)
    pool_type = pltpu.VMEM((2, DEEP, *packed.shape[1:]), bf16)

    def branch(number):
        caps = PLANS[number]
        spare = 2 * DEEP * 4 - max(sum(caps[: line // 2]), sum(caps[line // 2 :]))
        spare = spare - EASE if spare > 4 * EASE else spare
        cuts = (spare // 32 * 16, (spare + 16) // 32 * 16)

        def run(hidden_states, norm_gain, ids, weights, w_gate, w_up, w_down, kv, packed, lengths):
            moe_out, cache, other_pool = pl.pallas_call(
                functools.partial(fused_kernel, sizes, caps, cuts),
                out_shape=(
                    pltpu.VMEM((rows, model_width), bf16),
                    pltpu.VMEM((layers, slots, line * block, width), bf16),
                    pool_type,
                ),
                in_specs=[in_vmem] * 7 + [in_hbm, in_vmem],
                out_specs=(in_vmem,) * 3,
                scratch_shapes=[
                    pltpu.VMEM((plane, chips, 2, rows, model_width), bf16),
                    pltpu.VMEM((plane, chips, 2, rows, LANES), jnp.float32),
                    pltpu.VMEM((plane, chips, 2, rows, model_width), bf16),
                    pltpu.VMEM((plane, chips, 2, rows, model_width), bf16),
                    pltpu.VMEM((chips, 2, rows, model_width), jnp.float32),
                    pltpu.VMEM((chips, rows, model_width), jnp.float32),
                    pltpu.VMEM((2, rows, model_width), jnp.float32),
                    pltpu.VMEM((2, rows, model_width), jnp.float32),
                    pltpu.VMEM((rows, model_width), bf16),
                    pltpu.VMEM((rows, model_width), bf16),
                    pltpu.VMEM((line // 2 * slots, max(16, cuts[0]), width), bf16),
                    pltpu.VMEM((line // 2 * slots, max(16, cuts[1]), width), bf16),
                    dma((rounds, line // 2)),
                    dma((rounds, line // 2)),
                    dma((rounds, line // 2)),
                    dma((rounds, line // 2)),
                    dma,
                    dma((2 * DEEP,)),
                    dma((2, DEEP)),
                    dma((2, DEEP)),
                    dma((2, DEEP)),
                    dma((2, DEEP)),
                    dma((2,)),
                    dma((2,)),
                    dma((2, line // 2)),
                    dma((2, line // 2)),
                    dma((2, 3)),
                    dma((2, 3)),
                    dma((2,)),
                    dma((2,)),
                    dma((2, plane)),
                    dma((2, plane)),
                    dma((plane,)),
                    dma((plane,)),
                    dma,
                    dma,
                    dma,
                    dma,
                    dma,
                    dma,
                ],
                compiler_params=pltpu.CompilerParams(
                    collective_id=number, has_side_effects=True, vmem_limit_bytes=15 * 1024 * 1024
                ),
            )(hidden_states, norm_gain, ids, weights, w_gate, w_up, w_down, kv, packed)
            return mask_cache(lengths, cache, other_pool, moe_out, heads, block)

        return run

    cache, moe_out = lax.switch(
        chosen[0],
        [branch(number) for number in range(len(PLANS))],
        hidden_states, norm_gain, expert_ids.T, route_weights.T, w_gate, w_up, w_down, kv, packed, lengths,
    )
    return (moe_out, cache)


def solution(mesh):
    sizes = tuple(mesh.shape[name] for name in ("group", "tensor", "seq"))

    def shards(hidden_states, *rest):
        tokens = hidden_states.shape[0] * sizes[0] * sizes[1] * sizes[2]
        one_expert = rest[3].shape[0] == 1 and sizes[0] * sizes[1] <= LANES
        layers, requests, heads, block, width = rest[6].shape
        regular = layers == 2 and requests == 2 * LINE and heads * requests == 8 * LINE and block == 8 * UNIT
        if tokens <= DENSE_TOKENS and one_expert and sizes == (2, LINE, 2) and regular:
            return fused_shards(sizes, hidden_states, *rest)
        return routed_shards(hidden_states, *rest)

    return jax.shard_map(
        shards,
        mesh=mesh,
        in_specs=(
            P(("group", "tensor", "seq"), None),
            P(),
            P(("group", "tensor", "seq"), None),
            P(("group", "tensor", "seq"), None),
            P(("group", "tensor"), None, "seq"),
            P(("group", "tensor"), None, "seq"),
            P(("group", "tensor"), "seq", None),
            P("seq", None, None, ("group", "tensor"), None),
            P(),
        ),
        out_specs=(P(("group", "tensor", "seq"), None), P("seq", "tensor", "group", None)),
        check_vma=False,
    )
```

```python
import functools
import jax
import jax.numpy as jnp
from jax import lax
from jax.experimental import pallas as pl
from jax.experimental.pallas import tpu as pltpu
from jax.sharding import PartitionSpec as P

epsilon = 1e-06
LANES = 128
DENSE_TOKENS = 1024
WINDOW = 3
LINE = 8
RELAY_LAG = 3
SHARE_LAG = 4
LAST_LAG = 6
EASE = 16
UNIT = 32
DEEP = 32
PLANS = (
    (48, 48, 40, 40, 56, 48, 40, 32),
    (48, 48, 48, 48, 56, 56, 44, 32),
    (56, 48, 48, 40, 56, 56, 44, 32),
    (56, 56, 48, 48, 64, 56, 44, 32),
    (56, 56, 56, 56, 64, 60, 56, 44),
    (64, 64, 64, 64, 64, 64, 64, 64),
)
MESH = pl.DeviceIdType.MESH


def hand_over(prefill_key_value, lengths):
    layers_here, requests, heads, block, width = prefill_key_value.shape
    block_index = lax.axis_index("group") * lax.axis_size("tensor") + lax.axis_index("tensor")
    positions = block_index * block + jnp.arange(block, dtype=jnp.int32)
    keep = positions[None, :] < lengths[:, None]
    masked_entries = jnp.where(
        keep[None, :, None, :, None], prefill_key_value, jnp.zeros((), prefill_key_value.dtype)
    )
    flat = masked_entries.reshape(layers_here, requests * heads, block, width)
    return lax.all_to_all(flat, "tensor", split_axis=1, concat_axis=2, tiled=True)


def mixture(hidden_states, norm_gain, expert_ids, route_weights, w_gate, w_up, w_down):
    wide = hidden_states.astype(jnp.float32)
    scale = lax.rsqrt(jnp.mean(wide * wide, axis=1, keepdims=True) + epsilon)
    normed = (wide * scale * norm_gain.astype(jnp.float32)).astype(jnp.bfloat16)
    share = route_weights / jnp.sum(route_weights, axis=1, keepdims=True)
    expert_local, model_width, part_width = w_gate.shape
    sources = lax.axis_size("group") * lax.axis_size("tensor")
    experts = expert_local * sources
    rows_here, top_count = expert_ids.shape
    most = min(rows_here, max(2, 2 * rows_here * top_count // experts))
    flat_ids = expert_ids.reshape(-1)
    expert_grid = jnp.arange(experts, dtype=jnp.int32)
    onehot = (flat_ids[:, None] == expert_grid[None, :]).astype(jnp.int32)
    choices = jnp.arange(flat_ids.shape[0], dtype=jnp.int32)
    before = (choices[:, None] > choices[None, :]).astype(jnp.float32)
    earlier = jnp.dot(before, onehot.astype(jnp.float32), preferred_element_type=jnp.float32).astype(jnp.int32)
    position = jnp.sum(earlier * onehot, axis=1)
    target = flat_ids * most + position
    slot_grid = jnp.arange(experts * most, dtype=jnp.int32)
    hits = (target[:, None] == slot_grid[None, :]).reshape(rows_here, top_count, experts * most)
    select = jnp.sum(hits.astype(jnp.float32), axis=1).astype(jnp.bfloat16)
    mixing = jnp.sum(jnp.where(hits, share[:, :, None], 0.0), axis=1)
    outgoing = lax.dot_general(
        select, normed, (((0,), (0,)), ((), ())), preferred_element_type=jnp.float32
    )
    outgoing = outgoing.astype(jnp.bfloat16).reshape(experts, most, model_width)
    arrived = lax.all_to_all(outgoing, ("group", "tensor"), split_axis=0, concat_axis=0, tiled=True)
    arrived = arrived.reshape(sources, expert_local, most, model_width)
    pooled = lax.all_gather(arrived, "seq", axis=0, tiled=True)
    gate = jnp.einsum("semd,edf->semf", pooled, w_gate, preferred_element_type=jnp.float32)
    upper = jnp.einsum("semd,edf->semf", pooled, w_up, preferred_element_type=jnp.float32)
    active = (jax.nn.silu(gate) * upper).astype(jnp.bfloat16)
    summed = lax.psum_scatter(
        jnp.einsum("semf,efd->semd", active, w_down, preferred_element_type=jnp.float32).astype(
            jnp.bfloat16
        ),
        "seq",
        scatter_dimension=0,
        tiled=True,
    )
    returned = lax.all_to_all(
        summed.reshape(sources * expert_local, most, model_width),
        ("group", "tensor"),
        split_axis=0,
        concat_axis=0,
        tiled=True,
    )
    flat_back = returned.reshape(experts * most, model_width).astype(jnp.float32)
    mixed = jnp.dot(mixing, flat_back, precision=lax.Precision.HIGHEST)
    return mixed.astype(jnp.bfloat16)


def routed_shards(
    hidden_states, norm_gain, expert_ids, route_weights, w_gate, w_up, w_down, prefill_key_value, lengths
):
    moe_out = mixture(hidden_states, norm_gain, expert_ids, route_weights, w_gate, w_up, w_down)
    decoder_slot_cache = hand_over(prefill_key_value, lengths)
    return (moe_out, decoder_slot_cache)


def fused_kernel(
    sizes, caps, cuts,
    hidden_ref, gain_ref, ids_ref, weights_ref, gate_w, up_w, down_w, kv_ref, packed_ref,
    moe_ref, cache_ref, other_pool_ref,
    tokens, mixes, partial, gathered, folded, swapped, mate_out, mate_in, outgoing, returned,
    lend_first, lend_last,
    near_send, near_recv, far_send, far_recv, own_sem,
    stream_send, stream_recv, relay_send, share_send, share_recv, lend_send, lend_recv, lent_send, lent_recv,
    line_send, line_recv, pair_send, pair_recv, plane_send, plane_recv,
    part_send, part_recv, swap_send, swap_recv, mate_send, mate_recv, back_send, back_recv,
):
    groups, line, seqs = sizes
    plane = groups * seqs
    g, t, s = lax.axis_index("group"), lax.axis_index("tensor"), lax.axis_index("seq")
    here = g * seqs + s
    chips = line // 2
    chip, core = t // 2, lax.rem(t, 2)
    pair = (g, t + 1 - 2 * core, s)
    mate = chip + 1 - 2 * lax.rem(chip, 2)
    across, mate_across = lax.rem(chip + 2, chips), lax.rem(mate + 2, chips)
    mate_device, across_device = (g, mate * 2 + core, s), (g, across * 2 + core, s)
    layers, slots_all, block, _ = kv_ref.shape
    slots = slots_all // line
    rounds = layers * slots
    half_line = line // 2
    half, seat = t // half_line, lax.rem(t, half_line)
    far_half = 1 - half

    def in_line(step):
        other = lax.rem(t + step, line)
        return other, (g, other, s)

    def in_plane(step):
        other = lax.rem(here + step, plane)
        return other, (other // seqs, t, lax.rem(other, seqs))

    barrier = pltpu.get_barrier_semaphore()
    for step in range(1, line):
        pl.semaphore_signal(barrier, inc=1, device_id=in_line(step)[1], device_id_type=MESH)
    for step in range(1, plane):
        pl.semaphore_signal(barrier, inc=1, device_id=in_plane(step)[1], device_id_type=MESH)
    for k in range(half_line):
        pl.semaphore_signal(
            barrier, inc=1, device_id=(1 - g, far_half * half_line + k, s), device_id_type=MESH
        )

    columns = pl.ds(pl.multiple_of(t * block, block), block)
    own = pltpu.make_async_copy(
        kv_ref.at[:, pl.ds(t * slots, slots)], cache_ref.at[:, :, columns], own_sem
    )
    own.start()

    wide = hidden_ref[...].astype(jnp.float32)
    scale = lax.rsqrt(jnp.mean(wide * wide, axis=1, keepdims=True) + epsilon)
    tokens[here, chip, core] = (wide * scale * gain_ref[...].astype(jnp.float32)[None, :]).astype(jnp.bfloat16)
    top, rows = ids_ref.shape
    ids = ids_ref[...].T
    weights = weights_ref[...].T
    share = weights / jnp.sum(weights, axis=1, keepdims=True)
    lane = lax.broadcasted_iota(jnp.int32, (rows, LANES), 1)
    mix = jnp.zeros((rows, LANES), jnp.float32)
    for k in range(top):
        mix = mix + jnp.where(lane == ids[:, k : k + 1], share[:, k : k + 1], 0.0)
    mixes[here, chip, core] = mix

    pl.semaphore_wait(barrier, line + plane - 2 + half_line)

    def cap_of(device):
        total = 0
        for k in range(line):
            total = total + jnp.where(device == k, caps[k], 0)
        return total

    cap = cap_of(t)
    inner = jnp.logical_or(chip == 1, chip == 2)
    first_chip, last_chip = 1 + far_half * 1, far_half * 3
    lane_index = lax.rem(chip, 2)

    def pool(side, lane, entry):
        start = pl.multiple_of((side * DEEP + entry) * UNIT, UNIT)
        return cache_ref.at[:, pl.ds(lane * (slots // 2), slots // 2), pl.ds(start, UNIT)]

    def near_copy(index, step):
        other = half * half_line + lax.rem(seat + step, half_line)
        layer, slot = index // slots, lax.rem(index, slots)
        return pltpu.make_async_remote_copy(
            src_ref=kv_ref.at[layer, other * slots + slot],
            dst_ref=cache_ref.at[layer, slot, columns],
            send_sem=near_send.at[index, step],
            recv_sem=near_recv.at[index, step],
            device_id=(g, other, s),
            device_id_type=MESH,
        )

    def far_copy(layer, index, k, source):
        other = far_half * half_line + k
        at, slot = index // slots, lax.rem(index, slots)
        kept = block - cuts[layer]
        return pltpu.make_async_remote_copy(
            src_ref=kv_ref.at[at, other * slots + slot, pl.ds(0, kept)],
            dst_ref=cache_ref.at[at, slot, pl.ds(pl.multiple_of(t * block, block), kept)],
            send_sem=far_send.at[index, k],
            recv_sem=far_recv.at[index, source],
            device_id=(g, other, s),
            device_id_type=MESH,
        )

    def both_before(place, amount):
        return jnp.minimum(place, 2 * DEEP - amount)

    def entry_at(place, amount):
        rest = place - (2 * DEEP - amount)
        single = amount - DEEP
        swapped_turns = jnp.where(lax.rem(rest, 2) == 0, DEEP + rest // 2, rest // 2)
        head = single // 2
        turn = rest - head
        later = jnp.where(lax.rem(turn, 3) == 2, head + turn // 3, DEEP + turn - turn // 3)
        in_order = jnp.where(rest < head, rest, later)
        one = jnp.where(amount == 2 * DEEP, swapped_turns, in_order)
        return jnp.where(rest < 0, place + single, one)

    def stream_copy(place):
        entry = entry_at(place, cap)
        first = entry < DEEP
        target = jnp.where(first, entry, entry - (cap - DEEP))
        return pltpu.make_async_remote_copy(
            src_ref=packed_ref.at[entry],
            dst_ref=pool(half, lane_index, target),
            send_sem=stream_send.at[entry],
            recv_sem=stream_recv.at[lane_index, target],
            device_id=(g, jnp.where(first, first_chip, last_chip) * 2 + core, s),
            device_id_type=MESH,
        )

    def share_copy(lane, entry):
        return pltpu.make_async_remote_copy(
            src_ref=pool(far_half, lane, entry), dst_ref=other_pool_ref.at[lane, entry],
            send_sem=share_send.at[lane, entry], recv_sem=share_recv.at[lane, entry],
            device_id=pair, device_id_type=MESH,
        )

    def relay_copy(lane, entry, target):
        return pltpu.make_async_remote_copy(
            src_ref=pool(far_half, lane, entry), dst_ref=pool(far_half, lane, target),
            send_sem=relay_send.at[lane, entry], recv_sem=stream_recv.at[lane, target],
            device_id=mate_device, device_id_type=MESH,
        )

    def span_of(amount, index):
        at = jnp.clip(index, 0, rounds)
        after = jnp.clip(index + 1, 0, rounds)
        return amount * at // rounds, amount * after // rounds

    lends = [buffer for buffer in (lend_first, lend_last)]

    def lend_copy(layer):
        cut = cuts[layer]
        return pltpu.make_async_remote_copy(
            src_ref=kv_ref.at[layer, pl.ds(far_half * half_line * slots, half_line * slots), pl.ds(block - cut, cut)],
            dst_ref=lends[layer],
            send_sem=lend_send.at[layer], recv_sem=lend_recv.at[layer],
            device_id=(1 - g, t, s), device_id_type=MESH,
        )

    def lent_copy(layer, k, source):
        cut = cuts[layer]
        start = pl.multiple_of(t * block + block - cut, 16)
        return pltpu.make_async_remote_copy(
            src_ref=lends[layer].at[pl.ds(k * slots, slots)],
            dst_ref=cache_ref.at[layer, :, pl.ds(start, cut)],
            send_sem=lent_send.at[layer, k], recv_sem=lent_recv.at[layer, source],
            device_id=(1 - g, far_half * half_line + k, s), device_id_type=MESH,
        )

    lent_layers = [layer for layer in range(layers) if cuts[layer] > 0]

    def far_each(index, source, act):
        if cuts[0] == cuts[1]:
            for k in range(half_line):
                act(far_copy(0, index, k, k if source is None else source))
            return
        for layer in range(layers):
            @pl.when(index // slots == layer)
            def _():
                for k in range(half_line):
                    act(far_copy(layer, index, k, k if source is None else source))

    pace = 2 if min(caps) == 2 * DEEP else 3

    def near_span(index):
        return jnp.minimum(pace * index // 2, rounds), jnp.minimum(pace * (index + 1) // 2, rounds)

    def kv_start(index):
        @pl.loop(*near_span(index))
        def _(turn):
            for step in range(1, half_line):
                near_copy(turn, step).start()

        @pl.when(g == 0)
        def _():
            far_each(index, seat, lambda copy: copy.start())

        @pl.when(g == 1)
        def _():
            @pl.loop(*span_of(cap, index))
            def _(place):
                stream_copy(place).start()

    def kv_sent(index):
        @pl.loop(*near_span(index))
        def _(turn):
            for step in range(1, half_line):
                near_copy(turn, step).wait_send()

        @pl.when(g == 0)
        def _():
            far_each(index, seat, lambda copy: copy.wait_send())

        @pl.when(g == 1)
        def _():
            @pl.loop(*span_of(cap, index))
            def _(place):
                stream_copy(place).wait_send()

    def arrivals(index):
        @pl.when(g == 1)
        def _():
            for i in range(2):
                amount = cap_of(far_half * half_line + 2 * i + core)

                @pl.when(inner)
                def _():
                    low, high = span_of(amount, index - RELAY_LAG)

                    @pl.loop(both_before(low, amount), both_before(high, amount))
                    def _(place):
                        relay_copy(i, place + amount - DEEP, place + amount - DEEP).wait_recv()
                        relay_copy(i, place + amount - DEEP, place).start()

                @pl.loop(*span_of(amount, index - SHARE_LAG))
                def _(place):
                    entry = entry_at(place, amount)

                    @pl.when(jnp.logical_and(inner, entry < DEEP))
                    def _():
                        @pl.when(entry < amount - DEEP)
                        def _():
                            relay_copy(i, entry, entry).wait_recv()

                        share_copy(i, entry).start()

                    @pl.when(jnp.logical_and(jnp.logical_not(inner), entry >= DEEP))
                    def _():
                        at = entry - (amount - DEEP)
                        relay_copy(i, at, at).wait_recv()
                        share_copy(i, at).start()

                @pl.when(jnp.logical_not(inner))
                def _():
                    low, high = span_of(amount, index - LAST_LAG)

                    @pl.loop(both_before(low, amount), both_before(high, amount))
                    def _(place):
                        relay_copy(i, place, place).wait_recv()
                        share_copy(i, place).start()

    def line_copies(stage, place, device):
        return [
            pltpu.make_async_remote_copy(
                src_ref=ref.at[here, place, core], dst_ref=ref.at[here, place, core],
                send_sem=line_send.at[i, stage], recv_sem=line_recv.at[i, stage],
                device_id=device, device_id_type=MESH,
            )
            for i, ref in enumerate((tokens, mixes))
        ]

    over_copies = line_copies(0, chip, across_device)
    mate_copies = line_copies(1, chip, mate_device)
    relay_copies = line_copies(2, across, mate_device)

    pair_copies = [
        pltpu.make_async_remote_copy(
            src_ref=ref.at[here, :, core], dst_ref=ref.at[here, :, core],
            send_sem=pair_send.at[i], recv_sem=pair_recv.at[i],
            device_id=pair, device_id_type=MESH,
        )
        for i, ref in enumerate((tokens, mixes))
    ]

    swap = pltpu.make_async_remote_copy(
        src_ref=folded.at[:, 1 - core], dst_ref=swapped,
        send_sem=swap_send, recv_sem=swap_recv,
        device_id=pair, device_id_type=MESH,
    )

    def plane_copies(step):
        other, device = in_plane(step)
        return [
            pltpu.make_async_remote_copy(
                src_ref=ref.at[here], dst_ref=ref.at[here],
                send_sem=plane_send.at[i, step], recv_sem=plane_recv.at[i, step],
                device_id=device, device_id_type=MESH,
            )
            for i, ref in enumerate((tokens, mixes))
        ]

    def part_copy(step):
        other, device = in_plane(step)
        return pltpu.make_async_remote_copy(
            src_ref=partial.at[other], dst_ref=gathered.at[step],
            send_sem=part_send.at[step], recv_sem=part_recv.at[step],
            device_id=device, device_id_type=MESH,
        )

    mate_swap = pltpu.make_async_remote_copy(
        src_ref=mate_out, dst_ref=mate_in, send_sem=mate_send, recv_sem=mate_recv,
        device_id=mate_device, device_id_type=MESH,
    )
    back = pltpu.make_async_remote_copy(
        src_ref=outgoing, dst_ref=returned, send_sem=back_send, recv_sem=back_recv,
        device_id=across_device, device_id_type=MESH,
    )

    for copy in over_copies + mate_copies:
        copy.start()

    @pl.when(g == 0)
    def _():
        for layer in lent_layers:
            lend_copy(layer).start()

    spread = [c for step in range(1, plane) for c in plane_copies(step)]
    expert = g * line + t
    width = tokens.shape[-1]
    count = line * rows

    def across_done():
        for copy in over_copies:
            copy.wait()
        for copy in relay_copies:
            copy.start()

    def line_done():
        @pl.when(g == 1)
        def _():
            for layer in lent_layers:
                lend_copy(layer).wait_recv()
                for k in range(half_line):
                    lent_copy(layer, k, seat).start()

        for copy in mate_copies + relay_copies:
            copy.wait()
        for copy in pair_copies:
            copy.start()

    def pair_done():
        for copy in pair_copies:
            copy.wait()
        for copy in spread:
            copy.start()

    def spread_done():
        for copy in spread:
            copy.wait()

        @pl.loop(0, plane)
        def _(quarter):
            x = tokens[quarter].reshape(count, width)
            gate = jnp.dot(x, gate_w[0], preferred_element_type=jnp.float32)
            upper = jnp.dot(x, up_w[0], preferred_element_type=jnp.float32)
            active = (gate / (1.0 + jnp.exp(-gate)) * upper).astype(jnp.bfloat16)
            mixed = mixes[quarter].reshape(count, LANES)
            places = lax.broadcasted_iota(jnp.int32, (count, LANES), 1)
            weight = jnp.sum(jnp.where(places == expert, mixed, 0.0), axis=1, keepdims=True)
            out = jnp.dot(active, down_w[0], preferred_element_type=jnp.float32) * weight
            partial[quarter] = out.astype(jnp.bfloat16).reshape(chips, 2, rows, width)

        for step in range(1, plane):
            part_copy(step).start()

    def parts_done():
        for step in range(1, plane):
            part_copy(step).wait()

        @pl.loop(0, chips)
        def _(place):
            for side in range(2):
                total = partial[here, place, side].astype(jnp.float32)
                for step in range(1, plane):
                    total = total + gathered[step, place, side].astype(jnp.float32)
                folded[place, side] = total

        swap.start()

    def swap_done():
        swap.wait()
        mate_out[0] = folded[mate, core] + swapped[mate]
        mate_out[1] = folded[mate_across, core] + swapped[mate_across]
        mate_swap.start()

    def mate_done():
        mate_swap.wait()
        outgoing[...] = (folded[across, core] + swapped[across] + mate_in[1]).astype(jnp.bfloat16)
        back.start()

    def back_done():
        back.wait()
        total = folded[chip, core] + swapped[chip] + mate_in[0] + returned[...].astype(jnp.float32)
        moe_ref[...] = total.astype(jnp.bfloat16)

    stages = (across_done, line_done, pair_done, spread_done, parts_done, swap_done, mate_done, back_done)

    @pl.loop(0, rounds + LAST_LAG)
    def _(index):
        for i, stage in enumerate(stages):
            pl.when(index == WINDOW + (rounds - WINDOW) * (i + 1) // 9)(stage)

        @pl.when(jnp.logical_and(index >= WINDOW, index < rounds))
        def _():
            kv_sent(index - WINDOW)

        @pl.when(index < rounds)
        def _():
            kv_start(index)

        arrivals(index)

    @pl.loop(rounds - WINDOW, rounds)
    def _(index):
        kv_sent(index)

    @pl.when(g == 0)
    def _():
        @pl.loop(0, rounds)
        def _(index):
            far_each(index, None, lambda copy: copy.wait_recv())

        for layer in lent_layers:
            lend_copy(layer).wait_send()
            for k in range(half_line):
                lent_copy(layer, k, k).wait_recv()

    @pl.loop(0, rounds)
    def _(index):
        for step in range(1, half_line):
            near_copy(index, step).wait_recv()

    @pl.when(g == 1)
    def _():
        for layer in lent_layers:
            for k in range(half_line):
                lent_copy(layer, k, seat).wait_send()

        @pl.loop(0, DEEP)
        def _(entry):
            for i in range(2):
                share_copy(i, entry).wait()

        @pl.when(inner)
        def _():
            for i in range(2):
                amount = cap_of(far_half * half_line + 2 * i + core)

                @pl.loop(amount - DEEP, DEEP)
                def _(entry):
                    relay_copy(i, entry, entry).wait_send()

    own.wait()


def units_of(length, start, block):
    return jnp.clip((length - start + UNIT - 1) // UNIT, 0, block // UNIT)


def pack_kernel(heads, lengths_ref, kv_ref, packed_ref, chosen_ref, sems):
    layers, slots_all, block, width = kv_ref.shape
    requests = slots_all // heads
    quarter = requests // 4
    g, t = lax.axis_index("group"), lax.axis_index("tensor")
    start = (g * LINE + t) * block
    far_half = jnp.where(t < LINE // 2, 1, 0)

    def each(act, last, cap):
        chip = 1 + far_half if last == 0 else 3 * far_half

        def request(r, before):
            number = chip * quarter + r
            amount = units_of(lengths_ref[number], start, block)

            @pl.loop(0, amount)
            def _(q):
                k = before + q
                entry = k if last == 0 else cap - 1 - k
                act(number, q, entry)

            return before + amount

        lax.fori_loop(0, quarter, request, jnp.int32(0))

    def copy(number, q, entry):
        return pltpu.make_async_copy(
            kv_ref.at[:, pl.ds(number * heads, heads), pl.ds(pl.multiple_of(q * UNIT, UNIT), UNIT)],
            packed_ref.at[entry],
            sems.at[entry],
        )

    @pl.when(g == 1)
    def _():
        each(lambda *a: copy(*a).start(), 0, 0)

    misses = [jnp.int32(0) for _ in PLANS]
    for device in range(LINE):
        first = requests // 2 if device < LINE // 2 else 0
        needed = jnp.int32(0)
        for number in range(first, first + requests // 2):
            needed = needed + units_of(lengths_ref[number], (LINE + device) * block, block)
        for i, plan in enumerate(PLANS):
            misses[i] = misses[i] + jnp.where(needed > plan[device], 1, 0)
    chosen = jnp.int32(len(PLANS) - 1)
    for i in reversed(range(len(PLANS) - 1)):
        chosen = jnp.where(misses[i] == 0, i, chosen)
    chosen_ref[0] = chosen
    cap = jnp.int32(0)
    for i, plan in enumerate(PLANS):
        mine = jnp.int32(0)
        for device in range(LINE):
            mine = mine + jnp.where(t == device, plan[device], 0)
        cap = cap + jnp.where(chosen == i, mine, 0)

    @pl.when(g == 1)
    def _():
        each(lambda *a: copy(*a).start(), 1, cap)
        each(lambda *a: copy(*a).wait(), 0, 0)
        each(lambda *a: copy(*a).wait(), 1, cap)


def pack(lengths, kv, heads):
    layers, slots_all, block, width = kv.shape
    in_smem = pl.BlockSpec(memory_space=pltpu.SMEM)
    return pl.pallas_call(
        functools.partial(pack_kernel, heads),
        out_shape=(
            pltpu.VMEM((2 * DEEP, layers, heads, UNIT, width), kv.dtype),
            jax.ShapeDtypeStruct((1,), jnp.int32),
        ),
        in_specs=[in_smem, pl.BlockSpec(memory_space=pl.ANY)],
        out_specs=(pl.BlockSpec(memory_space=pltpu.VMEM), in_smem),
        scratch_shapes=[pltpu.SemaphoreType.DMA((2 * DEEP,))],
        compiler_params=pltpu.CompilerParams(vmem_limit_bytes=1024 * 1024),
    )(lengths, kv)


def mask_kernel(
    heads, piece,
    lengths_ref, cache_ref, other_pool_ref, moe_ref,
    out_ref, moe_out_ref,
    zeros, zero_unit, edges, edge_units, sems, unit_sems, moe_sem,
):
    layers, slots, span, width = cache_ref.shape
    pieces = span // piece
    half_line = pieces // 2
    per_device = slots // heads
    per_block = piece // UNIT
    g, t = lax.axis_index("group"), lax.axis_index("tensor")
    base = g * span
    half, core, chip = t // half_line, lax.rem(t, 2), t // 2
    inner = jnp.logical_or(chip == 1, chip == 2)
    moe_copy = pltpu.make_async_copy(moe_ref, moe_out_ref, moe_sem)
    moe_copy.start()
    zeros[...] = jnp.zeros(zeros.shape, zeros.dtype)
    zero_unit[...] = jnp.zeros(zero_unit.shape, zero_unit.dtype)
    places = lax.broadcasted_iota(jnp.int32, (piece, width), 0)
    unit_places = lax.broadcasted_iota(jnp.int32, zero_unit.shape, 2)
    direct_low = jnp.where(g == 0, 0, half * half_line)
    direct_high = jnp.where(g == 0, pieces, half * half_line + half_line)

    def rows_of(index):
        return pl.ds(pl.multiple_of(index * piece, piece), piece)

    def target(layer, r, index):
        return out_ref.at[layer, pl.ds(r * heads, heads), rows_of(index)]

    def unit_target(r, source, q):
        start = pl.multiple_of(source * piece + q * UNIT, UNIT)
        return out_ref.at[:, pl.ds(r * heads, heads), pl.ds(start, UNIT)]

    @pl.loop(0, per_device)
    def _(r):
        length = lengths_ref[per_device * t + r] - base
        group = pl.ds(r * heads, heads)

        @pl.loop(direct_low, direct_high)
        def _(index):
            left = length - index * piece

            @pl.when(left >= piece)
            def _():
                for layer in range(layers):
                    source = cache_ref.at[layer, group, rows_of(index)]
                    pltpu.make_async_copy(source, target(layer, r, index), sems.at[layer, r, index]).start()

            @pl.when(left <= 0)
            def _():
                for layer in range(layers):
                    pltpu.make_async_copy(zeros, target(layer, r, index), sems.at[layer, r, index]).start()

            @pl.when(jnp.logical_and(left > 0, left < piece))
            def _():
                for layer in range(layers):
                    @pl.loop(0, heads)
                    def _(head):
                        edges[layer, r * heads + head] = jnp.where(
                            places < left,
                            cache_ref[layer, r * heads + head, rows_of(index)],
                            jnp.zeros((), edges.dtype),
                        )

                    edge = edges.at[layer, group]
                    pltpu.make_async_copy(edge, target(layer, r, index), sems.at[layer, r, index]).start()

    @pl.when(g == 1)
    def _():
        @pl.loop(0, half_line)
        def _(k):
            source = (1 - half) * half_line + k
            start = base + source * piece
            before = jnp.int32(0)
            for r in range(2 * per_device):
                number = chip * 2 * per_device + r
                length = lengths_ref[number] - start
                mine = r - core * per_device

                @pl.when(jnp.logical_and(mine >= 0, mine < per_device))
                def _():
                    @pl.loop(0, per_block)
                    def _(q):
                        left = length - q * UNIT
                        order = before + q
                        entry = jnp.where(inner, order, DEEP - 1 - order)
                        rows = ((1 - half) * DEEP + entry) * UNIT
                        own_unit = cache_ref.at[
                            :, pl.ds((k // 2) * (slots // 2), slots // 2), pl.ds(pl.multiple_of(rows, UNIT), UNIT)
                        ]
                        at = unit_target(mine, source, q)
                        sem = unit_sems.at[mine, k, q]
                        for which, unit in enumerate((own_unit, other_pool_ref.at[k // 2, entry])):
                            here = (lax.rem(k, 2) == core) if which == 0 else (lax.rem(k, 2) != core)

                            @pl.when(jnp.logical_and(here, left >= UNIT))
                            def _():
                                pltpu.make_async_copy(unit, at, sem).start()

                            @pl.when(jnp.logical_and(here, jnp.logical_and(left > 0, left < UNIT)))
                            def _():
                                edge_units[mine] = jnp.where(
                                    unit_places < left, unit[...], jnp.zeros((), edges.dtype)
                                )
                                pltpu.make_async_copy(edge_units.at[mine], at, sem).start()

                        @pl.when(left <= 0)
                        def _():
                            pltpu.make_async_copy(zero_unit, at, sem).start()

                before = before + units_of(lengths_ref[number], start, piece)

    @pl.loop(0, per_device)
    def _(r):
        @pl.loop(direct_low, direct_high)
        def _(index):
            for layer in range(layers):
                pltpu.make_async_copy(zeros, target(layer, r, index), sems.at[layer, r, index]).wait()

    @pl.when(g == 1)
    def _():
        @pl.loop(0, half_line)
        def _(k):
            source = (1 - half) * half_line + k
            for mine in range(per_device):
                @pl.loop(0, per_block)
                def _(q):
                    at = unit_target(mine, source, q)
                    pltpu.make_async_copy(zero_unit, at, unit_sems.at[mine, k, q]).wait()

    moe_copy.wait()


def mask_cache(lengths, cache, other_pool, moe, heads, piece):
    layers, slots, span, width = cache.shape
    in_smem = pl.BlockSpec(memory_space=pltpu.SMEM)
    in_vmem = pl.BlockSpec(memory_space=pltpu.VMEM)
    cache, other_pool, moe = (
        pltpu.with_memory_space_constraint(x, pltpu.VMEM) for x in (cache, other_pool, moe)
    )
    in_place = pl.BlockSpec(memory_space=pl.ANY)
    unit = (layers, heads, UNIT, width)
    pieces = span // piece
    return pl.pallas_call(
        functools.partial(mask_kernel, heads, piece),
        out_shape=(
            jax.ShapeDtypeStruct(cache.shape, cache.dtype),
            jax.ShapeDtypeStruct(moe.shape, moe.dtype),
        ),
        in_specs=[in_smem, in_vmem, in_vmem, in_vmem],
        out_specs=(in_place, in_place),
        scratch_shapes=[
            pltpu.VMEM((heads, piece, width), cache.dtype),
            pltpu.VMEM(unit, cache.dtype),
            pltpu.VMEM((layers, slots, piece, width), cache.dtype),
            pltpu.VMEM((slots // heads, *unit), cache.dtype),
            pltpu.SemaphoreType.DMA((layers, slots // heads, pieces)),
            pltpu.SemaphoreType.DMA((slots // heads, pieces // 2, piece // UNIT)),
            pltpu.SemaphoreType.DMA,
        ],
        compiler_params=pltpu.CompilerParams(vmem_limit_bytes=4 * 1024 * 1024),
    )(lengths, cache, other_pool, moe)


def fused_shards(
    sizes,
    hidden_states, norm_gain, expert_ids, route_weights, w_gate, w_up, w_down, prefill_key_value, lengths,
):
    groups, line, seqs = sizes
    plane, chips = groups * seqs, line // 2
    layers, requests, heads, block, width = prefill_key_value.shape
    rows, model_width = hidden_states.shape
    slots = requests * heads // line
    rounds = layers * slots
    bf16 = jnp.bfloat16
    dma = pltpu.SemaphoreType.DMA
    in_vmem = pl.BlockSpec(memory_space=pltpu.VMEM)
    in_hbm = pl.BlockSpec(memory_space=pl.ANY)
    kv = prefill_key_value.reshape(layers, requests * heads, block, width)

    packed, chosen = pack(lengths, kv, heads)
    pool_type = pltpu.VMEM((2, DEEP, *packed.shape[1:]), bf16)

    def branch(number):
        caps = PLANS[number]
        spare = 2 * DEEP * 4 - max(sum(caps[: line // 2]), sum(caps[line // 2 :]))
        spare = spare - EASE if spare > 4 * EASE else spare
        cuts = (spare // 32 * 16, (spare + 16) // 32 * 16)

        def run(hidden_states, norm_gain, ids, weights, w_gate, w_up, w_down, kv, packed, lengths):
            moe_out, cache, other_pool = pl.pallas_call(
                functools.partial(fused_kernel, sizes, caps, cuts),
                out_shape=(
                    pltpu.VMEM((rows, model_width), bf16),
                    pltpu.VMEM((layers, slots, line * block, width), bf16),
                    pool_type,
                ),
                in_specs=[in_vmem] * 7 + [in_hbm, in_vmem],
                out_specs=(in_vmem,) * 3,
                scratch_shapes=[
                    pltpu.VMEM((plane, chips, 2, rows, model_width), bf16),
                    pltpu.VMEM((plane, chips, 2, rows, LANES), jnp.float32),
                    pltpu.VMEM((plane, chips, 2, rows, model_width), bf16),
                    pltpu.VMEM((plane, chips, 2, rows, model_width), bf16),
                    pltpu.VMEM((chips, 2, rows, model_width), jnp.float32),
                    pltpu.VMEM((chips, rows, model_width), jnp.float32),
                    pltpu.VMEM((2, rows, model_width), jnp.float32),
                    pltpu.VMEM((2, rows, model_width), jnp.float32),
                    pltpu.VMEM((rows, model_width), bf16),
                    pltpu.VMEM((rows, model_width), bf16),
                    pltpu.VMEM((line // 2 * slots, max(16, cuts[0]), width), bf16),
                    pltpu.VMEM((line // 2 * slots, max(16, cuts[1]), width), bf16),
                    dma((rounds, line // 2)),
                    dma((rounds, line // 2)),
                    dma((rounds, line // 2)),
                    dma((rounds, line // 2)),
                    dma,
                    dma((2 * DEEP,)),
                    dma((2, DEEP)),
                    dma((2, DEEP)),
                    dma((2, DEEP)),
                    dma((2, DEEP)),
                    dma((2,)),
                    dma((2,)),
                    dma((2, line // 2)),
                    dma((2, line // 2)),
                    dma((2, 3)),
                    dma((2, 3)),
                    dma((2,)),
                    dma((2,)),
                    dma((2, plane)),
                    dma((2, plane)),
                    dma((plane,)),
                    dma((plane,)),
                    dma,
                    dma,
                    dma,
                    dma,
                    dma,
                    dma,
                ],
                compiler_params=pltpu.CompilerParams(
                    collective_id=number, has_side_effects=True, vmem_limit_bytes=15 * 1024 * 1024
                ),
            )(hidden_states, norm_gain, ids, weights, w_gate, w_up, w_down, kv, packed)
            return mask_cache(lengths, cache, other_pool, moe_out, heads, block)

        return run

    cache, moe_out = lax.switch(
        chosen[0],
        [branch(number) for number in range(len(PLANS))],
        hidden_states, norm_gain, expert_ids.T, route_weights.T, w_gate, w_up, w_down, kv, packed, lengths,
    )
    return (moe_out, cache)


def solution(mesh):
    sizes = tuple(mesh.shape[name] for name in ("group", "tensor", "seq"))

    def shards(hidden_states, *rest):
        tokens = hidden_states.shape[0] * sizes[0] * sizes[1] * sizes[2]
        one_expert = rest[3].shape[0] == 1 and sizes[0] * sizes[1] <= LANES
        layers, requests, heads, block, width = rest[6].shape
        regular = layers == 2 and requests == 2 * LINE and heads * requests == 8 * LINE and block == 8 * UNIT
        if tokens <= DENSE_TOKENS and one_expert and sizes == (2, LINE, 2) and regular:
            return fused_shards(sizes, hidden_states, *rest)
        return routed_shards(hidden_states, *rest)

    return jax.shard_map(
        shards,
        mesh=mesh,
        in_specs=(
            P(("group", "tensor", "seq"), None),
            P(),
            P(("group", "tensor", "seq"), None),
            P(("group", "tensor", "seq"), None),
            P(("group", "tensor"), None, "seq"),
            P(("group", "tensor"), None, "seq"),
            P(("group", "tensor"), "seq", None),
            P("seq", None, None, ("group", "tensor"), None),
            P(),
        ),
        out_specs=(P(("group", "tensor", "seq"), None), P("seq", "tensor", "group", None)),
        check_vma=False,
    )
```
